512 devices in a mesh: row: 8 (over y), col: 64 (over x, z, core).
Axes of the slice: x: 4, y: 8, z: 8, core: 2. Of those that a mesh axis runs over, the one named last changes fastest.
Arguments:
- phase_codes: int32 [256, 32768], P('row', 'col'), may hold values from 0 to 4095
- aperture: int32 [256, 32768], P('row', 'col'), may hold values from 0 to 1
- tile_offsets: int32 [16, 64], P('row', 'col'), may hold values from 0 to 4095
Outputs:
- psf_field: float32 [2, 256, 131072], P(None, 'row', 'col')
The draws below stay inside these ranges and needn't reach their ends.
All inputs are finite; a program needn't handle non-finite values.
Results may differ from the reference program's by a relative error of at most 0.00013.
Values sent between devices are 32-bit elements; how exact they have to be, the bound alone decides.
A program may use at most 64 MiB of HBM per device.

```python
import jax
import jax.numpy as jnp

NPUP = 32768
NPAD = 131072
ROWS = 256
LEVELS = 4096
TILE_R = 16
TILE_C = 512


def draw_aperture(key, part):
    column_pos = jnp.arange(NPUP, dtype=jnp.int32)
    row_pos = jnp.arange(ROWS, dtype=jnp.int32)
    column_part = 850 * column_pos // NPUP
    threshold = 150 + row_pos[:, None] * column_part[None, :] // ROWS
    uniform_draw = jax.random.randint(key, (ROWS, NPUP), 0, 1000, dtype=jnp.int32)
    return (uniform_draw < threshold).astype(jnp.int32)


def touch_ends(drawn, key, low, high):
    longest = drawn.shape.index(max(drawn.shape))
    spots = []
    for shift in (0, 1):
        where = [jax.random.randint(jax.random.fold_in(key, axis), (), 0, length) for axis, length in enumerate(drawn.shape)]
        where[longest] = (where[longest] + shift) % drawn.shape[longest]
        spots.append(tuple(where))
    return drawn.at[spots[0]].set(low).at[spots[1]].set(high)


def setup_inputs(seed: int = 0) -> dict:
    seeds = jax.random.split(jax.random.key(seed), 4)
    phase_codes = touch_ends(jax.random.randint(seeds[0], (ROWS, NPUP), 0, LEVELS), jax.random.fold_in(seeds[0], 1), 0, LEVELS - 1).astype(jnp.int32)
    aperture = draw_aperture(jax.random.fold_in(seeds[3], 71), 0)
    tile_offsets = touch_ends(jax.random.randint(seeds[2], (ROWS // TILE_R, NPUP // TILE_C), 0, LEVELS), jax.random.fold_in(seeds[2], 1), 0, LEVELS - 1).astype(jnp.int32)
    return {"phase_codes": phase_codes, "aperture": aperture, "tile_offsets": tile_offsets}


def reference(phase_codes, aperture, tile_offsets):
    tile_rows, tile_cols = tile_offsets.shape
    piston = jnp.cumsum(tile_offsets, axis=0) % LEVELS
    codes = phase_codes.reshape(tile_rows, TILE_R, tile_cols, TILE_C) + piston[:, None, :, None]
    codes = (codes % LEVELS).reshape(ROWS, NPUP)
    theta = codes.astype(jnp.float32) * (2.0 * jnp.pi / LEVELS)
    amplitude = aperture.astype(jnp.float32)
    field = amplitude * jnp.cos(theta) + 1j * (amplitude * jnp.sin(theta))
    spectrum = jnp.fft.fft(field, n=NPAD, axis=1)
    open_count = jnp.sum(aperture)
    scale = jnp.sqrt(jnp.float32(ROWS) / open_count.astype(jnp.float32))
    psf_field = jnp.stack([jnp.real(spectrum), jnp.imag(spectrum)]) * scale
    return psf_field.astype(jnp.float32)
```

```python
import functools
import math

import jax
import jax.numpy as jnp
from jax import lax
from jax.experimental import pallas as pl
from jax.experimental.pallas import tpu as pltpu
from jax.sharding import PartitionSpec as P

MESH = pl.DeviceIdType.MESH
F32, I32, BF16 = jnp.float32, jnp.int32, jnp.bfloat16

NY, NX, NZ, NCORE = 8, 4, 8, 2
NB = NX * NCORE
ROWS = 32
HALF = 16
GROUPS = 2
GROWS = HALF // GROUPS
CHUNKS = 4
CROWS = HALF // CHUNKS


def cos_sin(index, bits):
    size = 1 << bits
    index = index & (size - 1)
    quadrant = (index + (size >> 3)) >> (bits - 2)
    rest = index - (quadrant << (bits - 2))
    x = rest.astype(F32) * F32(2.0 * math.pi / size)
    y = x * x
    s = x * (1.0 + y * (-1.0 / 6 + y * (1.0 / 120 + y * (-1.0 / 5040 + y * (1.0 / 362880)))))
    c = 1.0 + y * (-0.5 + y * (1.0 / 24 + y * (-1.0 / 720 + y * (1.0 / 40320))))
    quadrant = quadrant & 3
    swap = (quadrant & 1) == 1
    cos = jnp.where(swap, s, c)
    sin = jnp.where(swap, c, s)
    cos = jnp.where((quadrant == 1) | (quadrant == 2), -cos, cos)
    sin = jnp.where(quadrant >= 2, -sin, sin)
    return cos, sin


def halves(value):
    high = value.astype(BF16)
    return high, (value - high.astype(F32)).astype(BF16)


def iota(shape, axis):
    return lax.broadcasted_iota(I32, shape, axis)


def rotation(cos, sin, part_out, part_in):
    cross = jnp.where(part_out == 0, sin, -sin)
    return jnp.where(part_out == part_in, cos, cross)


def kernel(codes, aperture, offsets, out, yslots, xslots, zslots, p1s, p1r, gathered,
           tcos, tsin, wmat, emat, zsend, zrecv, fsend,
           ysend, yrecv, axsend, axrecv, azsend, azrecv, p1send, p1recv,
           p2send, p2recv, asend, arecv, bsend, brecv):
    y = lax.axis_index("row")
    col = lax.axis_index("col")
    core = col % NCORE
    z = (col // NCORE) % NZ
    x = col // (NCORE * NZ)
    me = x * NCORE + core

    def at_y(k):
        return (k, col)

    def at_b(k):
        return (y, ((k // NCORE) * NZ + z) * NCORE + k % NCORE)

    def at_z(k):
        return (y, (x * NZ + k) * NCORE + core)

    def remote(src, dst, ss, rs, where):
        return pltpu.make_async_remote_copy(
            src_ref=src, dst_ref=dst, send_sem=ss, recv_sem=rs,
            device_id=where, device_id_type=MESH)

    barrier = pltpu.get_barrier_semaphore()

    @pl.loop(1, 8)
    def _(k):
        for where in (at_y((y + k) % NY), at_b((me + k) % NB), at_z((z + k) % NZ)):
            pl.semaphore_signal(barrier, inc=1, device_id=where, device_id_type=MESH)

    off0, off1 = offsets[0, 0], offsets[1, 0]
    opened = aperture[...]
    per_lane = jnp.sum(opened, axis=0, keepdims=True)
    count = sum(per_lane[:, j * 128:(j + 1) * 128] for j in range(4))
    yslots[y, 0:1, :] = jnp.full((1, 128), off0 + off1, I32)
    yslots[y, 1:2, :] = count

    row = iota((ROWS, 512), 0)
    code = codes[...] + jnp.where(row < 16, off0, off0 + off1)
    code = code & 4095
    marked = jnp.concatenate([(code >> 6) + 64 * opened, code & 63], axis=0)
    i, j = iota((512, 512), 0), iota((512, 512), 1)
    pick = jnp.where(i == 4 * (j & 127) + (j >> 7), 1.0, 0.0).astype(BF16)
    moved = jnp.dot(marked.astype(F32).astype(BF16), pick, preferred_element_type=F32)
    moved = moved.astype(I32)
    high, low = moved[:ROWS], moved[ROWS:]
    amplitude = (high >> 6).astype(F32)
    cos, sin = cos_sin(((high & 63) << 6) + low, 12)
    field = (amplitude * cos, amplitude * sin)
    for b in range(NB):
        bx, bc = b // NCORE, b % NCORE
        for part in range(2):
            p1s[b * 32 + part * 16:b * 32 + part * 16 + 16, :] = (
                field[part][bc * HALF:(bc + 1) * HALF, bx * 128:(bx + 1) * 128])

    pl.semaphore_wait(barrier, 21)

    def y_copy(peer):
        return remote(yslots.at[y], yslots.at[y], ysend.at[peer], yrecv.at[y], at_y(peer))

    def p1_copy(peer):
        return remote(p1s.at[pl.ds(peer * 32, 32), :], p1r.at[pl.ds(me * 32, 32), :],
                      p1send.at[peer], p1recv.at[me], at_b(peer))

    @pl.loop(1, 8)
    def _(k):
        y_copy((y + k) % NY).start()
        p1_copy((me + k) % NB).start()

    p1r[pl.ds(pl.multiple_of(me * 32, 32), 32), :] = p1s[pl.ds(pl.multiple_of(me * 32, 32), 32), :]

    @pl.loop(1, 8)
    def _(k):
        peer = (y + k) % NY
        remote(yslots.at[peer], yslots.at[peer], ysend.at[peer], yrecv.at[peer],
               at_y(peer)).wait_recv()

    before = jnp.zeros((1, 128), I32)
    count = jnp.zeros((1, 128), I32)
    for k in range(NY):
        before = before + jnp.where(k < y, yslots[k, 0:1, :], 0)
        count = count + yslots[k, 1:2, :]
    xslots[me, 0:1, :] = before & 4095
    xslots[me, 1:2, :] = count

    def ax_copy(peer):
        return remote(xslots.at[me], xslots.at[me], axsend.at[peer], axrecv.at[me], at_b(peer))

    @pl.loop(1, 8)
    def _(k):
        ax_copy((me + k) % NB).start()

    @pl.loop(1, 8)
    def _(k):
        peer = (me + k) % NB
        remote(p1s.at[pl.ds(peer * 32, 32), :], p1r.at[pl.ds(peer * 32, 32), :],
               p1send.at[peer], p1recv.at[peer], at_b(peer)).wait_recv()

    for n in range(HALF):
        for part in range(2):
            gathered[z, n, part * 8:(part + 1) * 8, :] = (
                p1r[pl.ds(part * 16 + n, NB, stride=32), :])

    right, left = (z + 1) % NZ, (z + NZ - 1) % NZ

    def ring(block, chunk, way, step):
        part = gathered.at[block, pl.ds(chunk * CROWS, CROWS)]
        return remote(part, part, p2send.at[way, step, chunk], p2recv.at[block, chunk],
                      at_z(right if way == 0 else left))

    def arrived(block, chunk):
        part = gathered.at[block, pl.ds(chunk * CROWS, CROWS)]
        remote(part, part, p2send.at[0, 0, chunk], p2recv.at[block, chunk],
               at_z(left)).wait_recv()

    for chunk in range(CHUNKS):
        ring(z, chunk, 0, 0).start()
        ring(z, chunk, 1, 0).start()

    @pl.loop(1, 8)
    def _(k):
        peer = (me + k) % NB
        remote(xslots.at[peer], xslots.at[peer], axsend.at[peer], axrecv.at[peer],
               at_b(peer)).wait_recv()
    zslots[z, 0:8, :] = xslots[:, 0, :]
    zslots[z, 8:16, :] = xslots[:, 1, :]

    def az_copy(peer):
        return remote(zslots.at[z], zslots.at[z], azsend.at[peer], azrecv.at[z], at_z(peer))

    @pl.loop(1, 8)
    def _(k):
        az_copy((z + k) % NZ).start()

    shape = (512, 128)
    i, j = iota(shape, 0), iota(shape, 1)
    source = j & 7
    a = ((source >> 1) * NZ + ((j >> 3) & 7)) * NCORE + (source & 1)
    cos, sin = cos_sin(a * (i & 255), 8)
    w_high, w_low = halves(rotation(cos, sin, i >> 8, j >> 6))
    wmat[:, 0:128] = w_high
    wmat[:, 128:256] = w_high
    wmat[:, 256:384] = w_low
    shape = (256, 128)
    cos, sin = cos_sin((4 * iota(shape, 1) + x) * iota(shape, 0), 17)
    tcos[...] = cos
    tsin[...] = sin
    shape = (32, 256)
    i, j = iota(shape, 0), iota(shape, 1)
    q = 2 * (i >> 3) + ((i >> 1) & 1)
    d_low = NCORE * z + ((i >> 2) & 1)
    cos, sin = cos_sin((4 * (j & 127) + x) * (8 * d_low + q), 9)
    e_high, e_low = halves(rotation(cos, sin, i & 1, j >> 7))
    emat[0:32, :] = e_high
    emat[32:64, :] = e_low

    for step in range(1, 4):
        for chunk in range(CHUNKS):
            for way in range(2):
                block = (z + NZ - step) % NZ if way == 0 else (z + step) % NZ
                arrived(block, chunk)
                if step < 3 or (chunk < CHUNKS // 2) == (way == 0):
                    ring(block, chunk, way, step).start()

    @pl.loop(1, 8)
    def _(k):
        peer = (z + k) % NZ
        remote(zslots.at[peer], zslots.at[peer], azsend.at[peer], azrecv.at[peer],
               at_z(peer)).wait_recv()
    pcos, psin = cos_sin(zslots[:, 0:8, :], 12)
    total = jnp.sum(zslots[:, 8:16, :], axis=0)
    total = jnp.sum(jnp.sum(total.astype(F32), axis=0, keepdims=True), axis=1, keepdims=True)
    scale = jnp.sqrt(F32(ROWS * NY) / total)

    for chunk in range(CHUNKS):
        arrived((z + 4) % NZ, chunk)

    nt = (((1,), (1,)), ((), ()))

    def a_copy(g, peer):
        return remote(zsend.at[g, :, pl.ds(peer * 8 * GROWS, 8 * GROWS), :], zrecv.at[x, g],
                      asend.at[g, peer], arecv.at[g, x], at_b(peer * NCORE + core))

    for g in range(GROUPS):
        @pl.loop(0, GROWS // 2)
        def _(pair, g=g):
            columns = []
            for n in range(2):
                block = gathered[:, g * GROWS + pair * 2 + n]
                re, im = block[:, 0:8, :], block[:, 8:16, :]
                columns.append(jnp.concatenate(
                    [(re * pcos - im * psin).reshape(64, 128),
                     (re * psin + im * pcos).reshape(64, 128)], axis=0))
            high, low = halves(jnp.concatenate(columns, axis=1))
            spec = jnp.dot(wmat[...], jnp.concatenate([high, low, high], axis=0),
                           preferred_element_type=F32)
            for n in range(2):
                re = spec[0:256, n * 128:(n + 1) * 128]
                im = spec[256:512, n * 128:(n + 1) * 128]
                c, s = tcos[...], tsin[...]
                turned = jnp.concatenate([re * c + im * s, im * c - re * s], axis=1)
                high, low = halves(turned)
                first = lax.dot_general(emat[...], high, nt, preferred_element_type=F32)
                second = lax.dot_general(emat[0:32, :], low, nt, preferred_element_type=F32)
                result = first[0:32] + first[32:64] + second
                for h in range(2):
                    zsend[g, h, pl.ds(pair * 2 + n, 32, stride=GROWS), :] = (
                        result[:, h * 128:(h + 1) * 128])

        for k in range(1, NX):
            a_copy(g, (x + k) % NX).start()
        zrecv[x, g] = zsend[g, :, pl.ds(pl.multiple_of(x * 8 * GROWS, 8 * GROWS), 8 * GROWS), :]

    def b_copy(g, peer):
        return remote(fsend.at[g, peer],
                      out.at[:, pl.ds(core * HALF + g * GROWS, GROWS), pl.ds(pl.multiple_of(x * 512, 512), 512)],
                      bsend.at[g, peer], brecv.at[g, me], at_b(peer))

    for g in range(GROUPS):
        for k in range(1, NX):
            peer = (x + k) % NX
            remote(zrecv.at[peer, g], zrecv.at[peer, g], asend.at[g, peer], arecv.at[g, peer],
                   at_b(peer * NCORE + core)).wait_recv()
        for dc in range(2):
            for qh in range(4):
                ql, h = qh // 2, qh % 2
                part = []
                for p in range(2):
                    start = ((dc * 2 + ql) * 2 + p) * GROWS
                    part.append([zrecv[b, g, h, start:start + GROWS, :] * scale for b in range(NX)])
                (r0, r1, r2, r3), (i0, i1, i2, i3) = part
                ar, ai, br, bi = r0 + r2, i0 + i2, r1 + r3, i1 + i3
                dr, di, er, ei = r0 - r2, i0 - i2, r1 - r3, i1 - i3
                results = ((ar + br, ai + bi), (dr + ei, di - er), (ar - br, ai - bi), (dr - ei, di + er))
                for dx in range(NX):
                    for p in range(2):
                        fsend[g, dx * NCORE + dc, p, :, qh * 128:(qh + 1) * 128] = results[dx][p]

        @pl.loop(1, 8)
        def _(k, g=g):
            b_copy(g, (me + k) % NB).start()
        out[:, pl.ds(pl.multiple_of(core * HALF + g * GROWS, GROWS), GROWS),
            pl.ds(pl.multiple_of(x * 512, 512), 512)] = fsend[g, me]

    for g in range(GROUPS):
        @pl.loop(1, 8)
        def _(k, g=g):
            peer = (me + k) % NB
            landing = out.at[:, pl.ds((peer % NCORE) * HALF + g * GROWS, GROWS),
                             pl.ds(pl.multiple_of((peer // NCORE) * 512, 512), 512)]
            remote(landing, landing, bsend.at[g, peer], brecv.at[g, peer], at_b(peer)).wait_recv()

    @pl.loop(1, 8)
    def _(k):
        y_copy((y + k) % NY).wait_send()
        p1_copy((me + k) % NB).wait_send()
        ax_copy((me + k) % NB).wait_send()
        az_copy((z + k) % NZ).wait_send()
        for g in range(GROUPS):
            b_copy(g, (me + k) % NB).wait_send()
    for step in range(4):
        for chunk in range(CHUNKS):
            for way in range(2):
                if step < 3 or (chunk < CHUNKS // 2) == (way == 0):
                    block = (z + NZ - step) % NZ if way == 0 else (z + step) % NZ
                    ring(block, chunk, way, step).wait_send()
    for g in range(GROUPS):
        for k in range(1, NX):
            a_copy(g, (x + k) % NX).wait_send()


def per_device(phase_codes, aperture, tile_offsets):
    dma = pltpu.SemaphoreType.DMA
    vmem = pltpu.VMEM
    return pl.pallas_call(
        kernel,
        out_shape=jax.ShapeDtypeStruct((2, ROWS, 2048), F32),
        in_specs=[pl.BlockSpec(memory_space=pltpu.VMEM),
                  pl.BlockSpec(memory_space=pltpu.VMEM),
                  pl.BlockSpec(memory_space=pltpu.SMEM)],
        out_specs=pl.BlockSpec(memory_space=pltpu.VMEM),
        scratch_shapes=[
            vmem((NY, 2, 128), I32), vmem((NB, 2, 128), I32), vmem((NZ, 16, 128), I32),
            vmem((NB * 32, 128), F32), vmem((NB * 32, 128), F32),
            vmem((NZ, HALF, 16, 128), F32),
            vmem((256, 128), F32), vmem((256, 128), F32),
            vmem((512, 384), BF16), vmem((64, 256), BF16),
            vmem((GROUPS, 2, 32 * GROWS, 128), F32),
            vmem((NX, GROUPS, 2, 8 * GROWS, 128), F32),
            vmem((GROUPS, NB, 2, GROWS, 512), F32),
            dma((NY,)), dma((NY,)), dma((NB,)), dma((NB,)), dma((NZ,)), dma((NZ,)),
            dma((NB,)), dma((NB,)),
            dma((2, 4, CHUNKS)), dma((NZ, CHUNKS)),
            dma((GROUPS, NX)), dma((GROUPS, NX)), dma((GROUPS, NB)), dma((GROUPS, NB)),
        ],
        compiler_params=pltpu.CompilerParams(collective_id=0, has_side_effects=True),
    )(phase_codes, aperture, tile_offsets)


def solution(mesh):
    placed = (P("row", "col"), P("row", "col"), P("row", "col"))
    return jax.shard_map(
        per_device, mesh=mesh, in_specs=placed, out_specs=P(None, "row", "col"), check_vma=False
    )
```

```python
import functools
import math

import jax
import jax.numpy as jnp
from jax import lax
from jax.experimental import pallas as pl
from jax.experimental.pallas import tpu as pltpu
from jax.sharding import PartitionSpec as P

MESH = pl.DeviceIdType.MESH
F32, I32, BF16 = jnp.float32, jnp.int32, jnp.bfloat16

NY, NX, NZ, NCORE = 8, 4, 8, 2
NB = NX * NCORE
ROWS = 32
HALF = 16
GROUPS = 4
GROWS = HALF // GROUPS


def cos_sin(index, bits):
    size = 1 << bits
    index = index & (size - 1)
    quadrant = (index + (size >> 3)) >> (bits - 2)
    rest = index - (quadrant << (bits - 2))
    x = rest.astype(F32) * F32(2.0 * math.pi / size)
    y = x * x
    s = x * (1.0 + y * (-1.0 / 6 + y * (1.0 / 120 + y * (-1.0 / 5040 + y * (1.0 / 362880)))))
    c = 1.0 + y * (-0.5 + y * (1.0 / 24 + y * (-1.0 / 720 + y * (1.0 / 40320))))
    quadrant = quadrant & 3
    swap = (quadrant & 1) == 1
    cos = jnp.where(swap, s, c)
    sin = jnp.where(swap, c, s)
    cos = jnp.where((quadrant == 1) | (quadrant == 2), -cos, cos)
    sin = jnp.where(quadrant >= 2, -sin, sin)
    return cos, sin


def halves(value):
    high = value.astype(BF16)
    return high, (value - high.astype(F32)).astype(BF16)


def iota(shape, axis):
    return lax.broadcasted_iota(I32, shape, axis)


def rotation(cos, sin, part_out, part_in):
    cross = jnp.where(part_out == 0, sin, -sin)
    return jnp.where(part_out == part_in, cos, cross)


def phase(name):
    pass


def kernel(codes_in, aperture_in, offsets_in, out, codes, aperture, offsets, yslots, xslots, zslots,
           p1s, p1r, gathered, tcos, tsin, wmat, emat, zsend, zrecv, fsend, landing,
           insem, ysend, yrecv, axsend, axrecv, azsend, azrecv, p1send, p1recv,
           p2send, p2recv, asend, arecv, bsend, brecv):
    y = lax.axis_index("row")
    col = lax.axis_index("col")
    core = col % NCORE
    z = (col // NCORE) % NZ
    x = col // (NCORE * NZ)
    me = x * NCORE + core

    def at_y(k):
        return (k, col)

    def at_b(k):
        return (y, ((k // NCORE) * NZ + z) * NCORE + k % NCORE)

    def at_z(k):
        return (y, (x * NZ + k) * NCORE + core)

    def remote(src, dst, ss, rs, where):
        return pltpu.make_async_remote_copy(
            src_ref=src, dst_ref=dst, send_sem=ss, recv_sem=rs,
            device_id=where, device_id_type=MESH)

    phase("start")
    barrier = pltpu.get_barrier_semaphore()

    @pl.loop(1, 8)
    def _(k):
        for where in (at_y((y + k) % NY), at_b((me + k) % NB), at_z((z + k) % NZ)):
            pl.semaphore_signal(barrier, inc=1, device_id=where, device_id_type=MESH)

    loads = [pltpu.make_async_copy(codes_in, codes, insem.at[0]),
             pltpu.make_async_copy(aperture_in, aperture, insem.at[1]),
             pltpu.make_async_copy(offsets_in, offsets, insem.at[2])]
    for load in loads:
        load.start()
    i, j = iota((512, 512), 0), iota((512, 512), 1)
    pick = jnp.where(i == 4 * (j & 127) + (j >> 7), 1.0, 0.0).astype(BF16)
    for load in loads:
        load.wait()

    phase("field")
    off0, off1 = offsets[:, 0:1], offsets[:, 1:2]
    opened = aperture[...]
    per_lane = jnp.sum(opened, axis=0, keepdims=True)
    count = sum(per_lane[:, j * 128:(j + 1) * 128] for j in range(4))
    yslots[y, 0:1, :] = jnp.broadcast_to(off0 + off1, (1, 128))
    yslots[y, 1:2, :] = count

    row = iota((ROWS, 512), 0)
    code = codes[...] + jnp.where(row < 16, off0, off0 + off1)
    code = code & 4095
    marked = jnp.concatenate([(code >> 6) + 64 * opened, code & 63], axis=0)
    moved = jnp.dot(marked.astype(F32).astype(BF16), pick, preferred_element_type=F32)
    moved = moved.astype(I32)
    high, low = moved[:ROWS], moved[ROWS:]
    amplitude = (high >> 6).astype(F32)
    cos, sin = cos_sin(((high & 63) << 6) + low, 12)
    field = (amplitude * cos, amplitude * sin)
    for b in range(NB):
        bx, bc = b // NCORE, b % NCORE
        for part in range(2):
            p1s[b * 32 + part * 16:b * 32 + part * 16 + 16, :] = (
                field[part][bc * HALF:(bc + 1) * HALF, bx * 128:(bx + 1) * 128])

    phase("barrier")
    pl.semaphore_wait(barrier, 21)

    phase("startp1")

    def y_copy(peer):
        return remote(yslots.at[y], yslots.at[y], ysend.at[peer], yrecv.at[y], at_y(peer))

    def p1_copy(peer):
        return remote(p1s.at[pl.ds(peer * 32, 32), :], p1r.at[pl.ds(me * 32, 32), :],
                      p1send.at[peer], p1recv.at[me], at_b(peer))

    @pl.loop(1, 8)
    def _(k):
        p1_copy((me + k) % NB).start()

    @pl.loop(1, 8)
    def _(k):
        y_copy((y + k) % NY).start()

    p1r[pl.ds(pl.multiple_of(me * 32, 32), 32), :] = p1s[pl.ds(pl.multiple_of(me * 32, 32), 32), :]

    phase("tables")
    shape = (512, 128)
    i, j = iota(shape, 0), iota(shape, 1)
    source = j & 7
    a = ((source >> 1) * NZ + ((j >> 3) & 7)) * NCORE + (source & 1)
    cos, sin = cos_sin(a * (i & 255), 8)
    w_high, w_low = halves(rotation(cos, sin, i >> 8, j >> 6))
    wmat[:, 0:128] = w_high
    wmat[:, 128:256] = w_high
    wmat[:, 256:384] = w_low
    shape = (256, 128)
    cos, sin = cos_sin((4 * iota(shape, 1) + x) * iota(shape, 0), 17)
    tcos[...] = cos
    tsin[...] = sin
    shape = (32, 256)
    i, j = iota(shape, 0), iota(shape, 1)
    q = 2 * (i >> 3) + ((i >> 1) & 1)
    d_low = NCORE * z + ((i >> 2) & 1)
    cos, sin = cos_sin((4 * (j & 127) + x) * (8 * d_low + q), 9)
    e_high, e_low = halves(rotation(cos, sin, i & 1, j >> 7))
    emat[0:32, :] = e_high
    emat[32:64, :] = e_low

    phase("p1wait")

    @pl.loop(1, 8)
    def _(k):
        peer = (me + k) % NB
        remote(p1s.at[pl.ds(peer * 32, 32), :], p1r.at[pl.ds(peer * 32, 32), :],
               p1send.at[peer], p1recv.at[peer], at_b(peer)).wait_recv()

    phase("relayout")
    for n in range(HALF):
        for part in range(2):
            gathered[z, n, part * 8:(part + 1) * 8, :] = (
                p1r[pl.ds(part * 16 + n, NB, stride=32), :])

    right, left = (z + 1) % NZ, (z + NZ - 1) % NZ

    def ring(block, group, way, step):
        part = gathered.at[block, pl.ds(group * GROWS, GROWS)]
        return remote(part, part, p2send.at[way, step, group], p2recv.at[block, group],
                      at_z(right if way == 0 else left))

    def ring_block(way, step):
        return (z + NZ - step) % NZ if way == 0 else (z + step) % NZ

    def forwards(way, step, group):
        return step < 3 or (group % 2 == 0) == (way == 0)

    def arrived(block, group):
        part = gathered.at[block, pl.ds(group * GROWS, GROWS)]
        remote(part, part, p2send.at[0, 0, group], p2recv.at[block, group],
               at_z(left)).wait_recv()

    def ring_step(step, group):
        for way in range(2):
            if step:
                arrived(ring_block(way, step), group)
            if forwards(way, step, group):
                ring(ring_block(way, step), group, way, step).start()

    def ax_copy(peer):
        return remote(xslots.at[me], xslots.at[me], axsend.at[peer], axrecv.at[me], at_b(peer))

    def az_copy(peer):
        return remote(zslots.at[z], zslots.at[z], azsend.at[peer], azrecv.at[z], at_z(peer))

    def small_y():
        @pl.loop(1, 8)
        def _(k):
            peer = (y + k) % NY
            remote(yslots.at[peer], yslots.at[peer], ysend.at[peer], yrecv.at[peer],
                   at_y(peer)).wait_recv()

        before = jnp.zeros((1, 128), I32)
        count = jnp.zeros((1, 128), I32)
        for k in range(NY):
            before = before + jnp.where(k < y, yslots[k, 0:1, :], 0)
            count = count + yslots[k, 1:2, :]
        xslots[me, 0:1, :] = before & 4095
        xslots[me, 1:2, :] = count

        @pl.loop(1, 8)
        def _(k):
            ax_copy((me + k) % NB).start()

    def small_x():
        @pl.loop(1, 8)
        def _(k):
            peer = (me + k) % NB
            remote(xslots.at[peer], xslots.at[peer], axsend.at[peer], axrecv.at[peer],
                   at_b(peer)).wait_recv()
        zslots[z, 0:8, :] = xslots[:, 0, :]
        zslots[z, 8:16, :] = xslots[:, 1, :]

        @pl.loop(1, 8)
        def _(k):
            az_copy((z + k) % NZ).start()

    known = []

    def small_z():
        @pl.loop(1, 8)
        def _(k):
            peer = (z + k) % NZ
            remote(zslots.at[peer], zslots.at[peer], azsend.at[peer], azrecv.at[peer],
                   at_z(peer)).wait_recv()
        total = jnp.sum(zslots[:, 8:16, :], axis=0)
        total = jnp.sum(jnp.sum(total.astype(F32), axis=0, keepdims=True), axis=1, keepdims=True)
        known.extend(cos_sin(zslots[:, 0:8, :], 12))
        known.append(jnp.sqrt(F32(ROWS * NY) / total))

    nt = (((1,), (1,)), ((), ()))

    def a_copy(g, peer):
        return remote(zsend.at[g, :, pl.ds(peer * 8 * GROWS, 8 * GROWS), :], zrecv.at[x, g],
                      asend.at[g, peer], arecv.at[g, x], at_b(peer * NCORE + core))

    def transform(g):
        pcos, psin = known[:2]
        for pair in range(GROWS // 2):
            columns = []
            for n in range(2):
                block = gathered[:, g * GROWS + pair * 2 + n]
                re, im = block[:, 0:8, :], block[:, 8:16, :]
                columns.append(jnp.concatenate(
                    [(re * pcos - im * psin).reshape(64, 128),
                     (re * psin + im * pcos).reshape(64, 128)], axis=0))
            high, low = halves(jnp.concatenate(columns, axis=1))
            spec = jnp.dot(wmat[...], jnp.concatenate([high, low, high], axis=0),
                           preferred_element_type=F32)
            for n in range(2):
                re = spec[0:256, n * 128:(n + 1) * 128]
                im = spec[256:512, n * 128:(n + 1) * 128]
                c, s = tcos[...], tsin[...]
                turned = jnp.concatenate([re * c + im * s, im * c - re * s], axis=1)
                high, low = halves(turned)
                first = lax.dot_general(emat[...], high, nt, preferred_element_type=F32)
                second = lax.dot_general(emat[0:32, :], low, nt, preferred_element_type=F32)
                result = first[0:32] + first[32:64] + second
                for h in range(2):
                    zsend[g, h, pl.ds(pair * 2 + n, 32, stride=GROWS), :] = (
                        result[:, h * 128:(h + 1) * 128])

    def finish(g):
        phase(f"fin{g}")
        arrived((z + 4) % NZ, g)
        if g == 0:
            phase("azwait")
            small_z()
        phase(f"dft{g}")
        transform(g)
        phase(f"asend{g}")
        for k in range(1, NX):
            a_copy(g, (x + k) % NX).start()
        zrecv[x, g] = zsend[g, :, pl.ds(pl.multiple_of(x * 8 * GROWS, 8 * GROWS), 8 * GROWS), :]

    def b_copy(g, peer):
        return remote(fsend.at[g, peer],
                      landing.at[core, g, :, pl.ds(pl.multiple_of(x * 512, 512), 512)],
                      bsend.at[g, peer], brecv.at[g, me], at_b(peer))

    def combine(g):
        phase(f"await{g}")
        for k in range(1, NX):
            peer = (x + k) % NX
            remote(zrecv.at[peer, g], zrecv.at[peer, g], asend.at[g, peer], arecv.at[g, peer],
                   at_b(peer * NCORE + core)).wait_recv()
        phase(f"dft4_{g}")
        scale = known[2]
        turn = jnp.where(iota((8, 128), 0) < GROWS, scale, -scale)
        for dc in range(2):
            for ql in range(2):
                for h in range(2):
                    start = (dc * 2 + ql) * 8
                    t = [zrecv[b, g, h, start:start + 8, :] for b in range(NX)]
                    even, odd = (t[0] + t[2]) * scale, (t[1] + t[3]) * scale
                    differ = (t[0] - t[2]) * scale
                    turned = pltpu.roll(t[1] - t[3], GROWS, axis=0) * turn
                    results = (even + odd, differ + turned, even - odd, differ - turned)
                    for dx in range(NX):
                        fsend[g, dx * NCORE + dc, :, (ql * 2 + h) * 128:(ql * 2 + h + 1) * 128] = results[dx]

        @pl.loop(1, 8)
        def _(k):
            b_copy(g, (me + k) % NB).start()
        landing[core, g, :, pl.ds(pl.multiple_of(x * 512, 512), 512)] = fsend[g, me]

    def deliver(g):
        phase(f"bwait{g}")

        @pl.loop(1, 8)
        def _(k):
            peer = (me + k) % NB
            spot = landing.at[peer % NCORE, g, :, pl.ds(pl.multiple_of((peer // NCORE) * 512, 512), 512)]
            remote(spot, spot, bsend.at[g, peer], brecv.at[g, peer], at_b(peer)).wait_recv()
        phase(f"out{g}")
        for c in range(NCORE):
            for p in range(2):
                out[p, c * HALF + g * GROWS:c * HALF + (g + 1) * GROWS, :] = (
                    landing[c, g, p * GROWS:(p + 1) * GROWS, :])

    for _, name, work in sorted(schedule(ring_step, finish, combine, deliver, small_y, small_x),
                                key=lambda e: e[0]):
        phase(name)
        work()

    phase("drain")

    @pl.loop(1, 8)
    def _(k):
        y_copy((y + k) % NY).wait_send()
        p1_copy((me + k) % NB).wait_send()
        ax_copy((me + k) % NB).wait_send()
        az_copy((z + k) % NZ).wait_send()
        for g in range(GROUPS):
            b_copy(g, (me + k) % NB).wait_send()
    for step in range(4):
        for g in range(GROUPS):
            for way in range(2):
                if forwards(way, step, g):
                    ring(ring_block(way, step), g, way, step).wait_send()
    for g in range(GROUPS):
        for k in range(1, NX):
            a_copy(g, (x + k) % NX).wait_send()
    phase(None)


def schedule(ring_step, finish, combine, deliver, small_y, small_x):
    hop, lag, fin, exch = PACE
    part = functools.partial
    events = [(SMALL[0], "ysmall", small_y), (SMALL[1], "xsmall", small_x)]
    for g in range(GROUPS):
        for step in range(4):
            events.append((hop * step + lag * g, f"r{step}{g}", part(ring_step, step, g)))
        done = hop * 4 + fin * g
        events.append((done, f"fin{g}", part(finish, g)))
        events.append((done + exch, f"await{g}", part(combine, g)))
        events.append((done + 2 * exch + 10.0, f"bwait{g}", part(deliver, g)))
    return events


PACE = (2.2, 1.0, 1.2, 5.0)
SMALL = (2.9, 5.3)


def per_device(phase_codes, aperture, tile_offsets):
    dma = pltpu.SemaphoreType.DMA
    vmem = pltpu.VMEM
    return pl.pallas_call(
        kernel,
        out_shape=pltpu.VMEM((2, ROWS, 2048), F32),
        in_specs=[pl.BlockSpec(memory_space=pl.ANY)] * 3,
        out_specs=pl.BlockSpec(memory_space=pltpu.VMEM),
        scratch_shapes=[
            vmem((ROWS, 512), I32), vmem((ROWS, 512), I32), vmem((1, 2), I32),
            vmem((NY, 2, 128), I32), vmem((NB, 2, 128), I32), vmem((NZ, 16, 128), I32),
            vmem((NB * 32, 128), F32), vmem((NB * 32, 128), F32),
            vmem((NZ, HALF, 16, 128), F32),
            vmem((256, 128), F32), vmem((256, 128), F32),
            vmem((512, 384), BF16), vmem((64, 256), BF16),
            vmem((GROUPS, 2, 32 * GROWS, 128), F32),
            vmem((NX, GROUPS, 2, 8 * GROWS, 128), F32),
            vmem((GROUPS, NB, 2 * GROWS, 512), F32),
            vmem((NCORE, GROUPS, 2 * GROWS, 2048), F32),
            dma((3,)),
            dma((NY,)), dma((NY,)), dma((NB,)), dma((NB,)), dma((NZ,)), dma((NZ,)),
            dma((NB,)), dma((NB,)),
            dma((2, 4, GROUPS)), dma((NZ, GROUPS)),
            dma((GROUPS, NX)), dma((GROUPS, NX)), dma((GROUPS, NB)), dma((GROUPS, NB)),
        ],
        compiler_params=pltpu.CompilerParams(collective_id=0, has_side_effects=True),
    )(phase_codes, aperture, tile_offsets.reshape(1, 2))


def solution(mesh):
    placed = (P("row", "col"), P("row", "col"), P("row", "col"))
    return jax.shard_map(
        per_device, mesh=mesh, in_specs=placed, out_specs=P(None, "row", "col"), check_vma=False
    )
```

```python
import functools
import math

import jax
import jax.numpy as jnp
from jax import lax
from jax.experimental import pallas as pl
from jax.experimental.pallas import tpu as pltpu
from jax.sharding import PartitionSpec as P

MESH = pl.DeviceIdType.MESH
F32, I32, BF16 = jnp.float32, jnp.int32, jnp.bfloat16

NY, NX, NZ, NCORE = 8, 4, 8, 2
NB = NX * NCORE
ROWS = 32
HALF = 16
MSG = 40
GROUPS = 4
GROWS = HALF // GROUPS


def cos_sin(index, bits):
    size = 1 << bits
    index = index & (size - 1)
    quadrant = (index + (size >> 3)) >> (bits - 2)
    rest = index - (quadrant << (bits - 2))
    x = rest.astype(F32) * F32(2.0 * math.pi / size)
    y = x * x
    s = x * (1.0 + y * (-1.0 / 6 + y * (1.0 / 120 + y * (-1.0 / 5040 + y * (1.0 / 362880)))))
    c = 1.0 + y * (-0.5 + y * (1.0 / 24 + y * (-1.0 / 720 + y * (1.0 / 40320))))
    quadrant = quadrant & 3
    swap = (quadrant & 1) == 1
    cos = jnp.where(swap, s, c)
    sin = jnp.where(swap, c, s)
    cos = jnp.where((quadrant == 1) | (quadrant == 2), -cos, cos)
    sin = jnp.where(quadrant >= 2, -sin, sin)
    return cos, sin


def halves(value):
    high = value.astype(BF16)
    return high, (value - high.astype(F32)).astype(BF16)


def iota(shape, axis):
    return lax.broadcasted_iota(I32, shape, axis)


def rotation(cos, sin, part_out, part_in):
    cross = jnp.where(part_out == 0, sin, -sin)
    return jnp.where(part_out == part_in, cos, cross)


def phase(name):
    pass


def kernel(codes_in, aperture_in, offsets_in, out, codes, aperture, offsets, yslots, zslots, cslots,
           p1s, p1r, gathered, tcos, tsin, wmat, emat, zsend, zrecv, fsend, landing,
           ready_y, ready_z, insem, p1send, p1recv, ysend, yrecv, azsend, azrecv, csend, crecv,
           p2send, p2recv, asend, arecv, bsend, brecv):
    y = lax.axis_index("row")
    col = lax.axis_index("col")
    core = col % NCORE
    z = (col // NCORE) % NZ
    x = col // (NCORE * NZ)
    me = x * NCORE + core

    def at_y(k):
        return (k, col)

    def at_b(k):
        return (y, ((k // NCORE) * NZ + z) * NCORE + k % NCORE)

    def at_z(k):
        return (y, (x * NZ + k) * NCORE + core)

    def remote(src, dst, ss, rs, where):
        return pltpu.make_async_remote_copy(
            src_ref=src, dst_ref=dst, send_sem=ss, recv_sem=rs,
            device_id=where, device_id_type=MESH)

    phase("start")
    barrier = pltpu.get_barrier_semaphore()

    def signal(semaphore, where):
        pl.semaphore_signal(semaphore, inc=1, device_id=where, device_id_type=MESH)

    partners = [((x + dx) % NX) * NCORE + (core + dc) % NCORE
                for dx, dc in ((2, 0), (2, 1), (1, 0), (3, 0), (1, 1), (3, 1), (0, 1))]
    right, left = (z + 1) % NZ, (z + NZ - 1) % NZ
    for peer in partners:
        signal(barrier, at_b(peer))
    for peer in (right, left):
        signal(barrier, at_z(peer))
    for k in range(2, NZ - 1):
        peer = (z + k) % NZ

        @pl.when(peer > z)
        def _():
            signal(barrier, at_z(peer))

    @pl.loop(y + 1, NY)
    def _(k):
        signal(barrier, at_y(k))

    loads = [pltpu.make_async_copy(codes_in, codes, insem.at[0]),
             pltpu.make_async_copy(aperture_in, aperture, insem.at[1]),
             pltpu.make_async_copy(offsets_in, offsets, insem.at[2])]
    for load in loads:
        load.start()
    i, j = iota((512, 512), 0), iota((512, 512), 1)
    pick = jnp.where(i == 4 * (j & 127) + (j >> 7), 1.0, 0.0).astype(BF16)
    for load in loads:
        load.wait()

    phase("field")
    off0, off1 = offsets[:, 0:1], offsets[:, 1:2]
    opened = aperture[...]
    per_lane = jnp.sum(opened, axis=0, keepdims=True)
    count = sum(per_lane[:, j * 128:(j + 1) * 128] for j in range(4))
    total = jnp.broadcast_to(off0 + off1, (1, 128)).astype(F32)
    count = count.astype(F32)

    row = iota((ROWS, 512), 0)
    code = codes[...] + jnp.where(row < 16, off0, off0 + off1)
    code = code & 4095
    marked = jnp.concatenate([(code >> 6) + 64 * opened, code & 63], axis=0)
    moved = jnp.dot(marked.astype(F32).astype(BF16), pick, preferred_element_type=F32)
    moved = moved.astype(I32)
    high, low = moved[:ROWS], moved[ROWS:]
    amplitude = (high >> 6).astype(F32)
    cos, sin = cos_sin(((high & 63) << 6) + low, 12)
    field = (amplitude * cos, amplitude * sin)
    for b in range(NB):
        bx, bc = b // NCORE, b % NCORE
        for part in range(2):
            p1s[b * MSG + part * 16:b * MSG + part * 16 + 16, :] = (
                field[part][bc * HALF:(bc + 1) * HALF, bx * 128:(bx + 1) * 128])
        p1s[b * MSG + 32:b * MSG + 33, :] = total
        p1s[b * MSG + 33:b * MSG + 34, :] = count

    phase("barrier")
    entered_z = z - (z + 6) // 7 - z // 7
    pl.semaphore_wait(barrier, 9 + entered_z + y)

    phase("startp1")

    def p1_copy(peer):
        return remote(p1s.at[pl.ds(peer * MSG, MSG), :], p1r.at[pl.ds(me * MSG, MSG), :],
                      p1send, p1recv, at_b(peer))

    for peer in partners:
        p1_copy(peer).start()
    for k in range(2, NZ - 1):
        peer = (z + k) % NZ

        @pl.when(peer < z)
        def _():
            signal(ready_z, at_z(peer))

    @pl.loop(0, y)
    def _(k):
        signal(ready_y, at_y(k))

    own = pl.ds(pl.multiple_of(me * MSG, MSG), MSG)
    p1r[own, :] = p1s[own, :]

    phase("tables")
    shape = (512, 128)
    i, j = iota(shape, 0), iota(shape, 1)
    source = j & 7
    a = ((source >> 1) * NZ + ((j >> 3) & 7)) * NCORE + (source & 1)
    cos, sin = cos_sin(a * (i & 255), 8)
    w_high, w_low = halves(rotation(cos, sin, i >> 8, j >> 6))
    wmat[:, 0:128] = w_high
    wmat[:, 128:256] = w_high
    wmat[:, 256:384] = w_low
    shape = (256, 128)
    cos, sin = cos_sin((4 * iota(shape, 1) + x) * iota(shape, 0), 17)
    tcos[...] = cos
    tsin[...] = sin
    shape = (32, 256)
    i, j = iota(shape, 0), iota(shape, 1)
    q = 2 * (i >> 3) + ((i >> 1) & 1)
    d_low = NCORE * z + ((i >> 2) & 1)
    cos, sin = cos_sin((4 * (j & 127) + x) * (8 * d_low + q), 9)
    e_high, e_low = halves(rotation(cos, sin, i & 1, j >> 7))
    emat[0:32, :] = e_high
    emat[32:64, :] = e_low

    phase("p1wait")
    seven = pl.ds(0, 7 * MSG)
    remote(p1s.at[seven, :], p1r.at[seven, :], p1send, p1recv, at_z(right)).wait_recv()

    phase("relayout")
    for n in range(HALF):
        for part in range(2):
            gathered[z, n, part * 8:(part + 1) * 8, :] = (
                p1r[pl.ds(part * 16 + n, NB, stride=MSG), :])

    def ring(block, group, way, step):
        part = gathered.at[block, pl.ds(group * GROWS, GROWS)]
        return remote(part, part, p2send, p2recv.at[block, group],
                      at_z(right if way == 0 else left))

    def ring_block(way, step):
        return (z + NZ - step) % NZ if way == 0 else (z + step) % NZ

    def forwards(way, step, group):
        return step < 3 or (group % 2 == 0) == (way == 0)

    def arrived(block, group):
        part = gathered.at[block, pl.ds(group * GROWS, GROWS)]
        remote(part, part, p2send, p2recv.at[block, group],
               at_z(left)).wait_recv()

    def ring_step(step, group):
        for way in range(2):
            if step:
                arrived(ring_block(way, step), group)
            if forwards(way, step, group):
                ring(ring_block(way, step), group, way, step).start()

    def y_copy(peer, slot):
        return remote(yslots.at[slot], yslots.at[slot], ysend.at[peer], yrecv.at[slot], at_y(peer))

    def az_copy(peer):
        return remote(zslots.at[z], zslots.at[z], azsend, azrecv, at_z(peer))

    def c_copy(peer):
        return remote(cslots.at[y], cslots.at[y], csend, crecv, at_y(peer))

    def small_y():
        yslots[y] = p1r[pl.ds(32, NB, stride=MSG), :]
        @pl.when(y < NY - 1)
        def _():
            pl.semaphore_wait(ready_y, NY - 1 - y)

        @pl.loop(y + 1, NY)
        def _(k):
            y_copy(k, y).start()

    def small_z():
        @pl.loop(0, y)
        def _(k):
            y_copy(k, k).wait_recv()
        before = lax.fori_loop(0, y, lambda k, acc: acc + yslots[k], jnp.zeros((NB, 128), F32))
        zslots[z, 0:8, :] = before
        zslots[z, 8:16, :] = p1r[pl.ds(33, NB, stride=MSG), :]
        @pl.when(z < NZ - 2)
        def _():
            pl.semaphore_wait(ready_z, 5 + (z + 6) // 7 - z)

        @pl.loop(1, NZ)
        def _(k):
            az_copy((z + k) % NZ).start()

    known = []

    def prefix():
        remote(zslots.at[pl.ds(0, 7)], zslots.at[pl.ds(0, 7)], azsend, azrecv, at_z(right)).wait_recv()
        known.extend(cos_sin(zslots[:, 0:8, :].astype(I32), 12))
        cslots[y] = jnp.sum(zslots[:, 8:16, :], axis=0)

        @pl.loop(1, NY)
        def _(k):
            c_copy((y + k) % NY).start()

    def normalization():
        remote(cslots.at[pl.ds(0, 7)], cslots.at[pl.ds(0, 7)], csend, crecv, at_z(right)).wait_recv()
        total = jnp.sum(cslots[...], axis=0)
        total = jnp.sum(jnp.sum(total, axis=0, keepdims=True), axis=1, keepdims=True)
        known.append(jnp.sqrt(F32(ROWS * NY) / total))

    nt = (((1,), (1,)), ((), ()))

    def a_copy(g, peer):
        return remote(zsend.at[g, :, pl.ds(peer * 8 * GROWS, 8 * GROWS), :], zrecv.at[x, g],
                      asend, arecv.at[g], at_b(peer * NCORE + core))

    def transform(g):
        pcos, psin = known[:2]
        for pair in range(GROWS // 2):
            columns = []
            for n in range(2):
                block = gathered[:, g * GROWS + pair * 2 + n]
                re, im = block[:, 0:8, :], block[:, 8:16, :]
                columns.append(jnp.concatenate(
                    [(re * pcos - im * psin).reshape(64, 128),
                     (re * psin + im * pcos).reshape(64, 128)], axis=0))
            high, low = halves(jnp.concatenate(columns, axis=1))
            spec = jnp.dot(wmat[...], jnp.concatenate([high, low, high], axis=0),
                           preferred_element_type=F32)
            for n in range(2):
                re = spec[0:256, n * 128:(n + 1) * 128]
                im = spec[256:512, n * 128:(n + 1) * 128]
                c, s = tcos[...], tsin[...]
                turned = jnp.concatenate([re * c + im * s, im * c - re * s], axis=1)
                high, low = halves(turned)
                first = lax.dot_general(emat[...], high, nt, preferred_element_type=F32)
                second = lax.dot_general(emat[0:32, :], low, nt, preferred_element_type=F32)
                result = first[0:32] + first[32:64] + second
                for h in range(2):
                    zsend[g, h, pl.ds(pair * 2 + n, 32, stride=GROWS), :] = (
                        result[:, h * 128:(h + 1) * 128])

    def finish(g):
        phase(f"fin{g}")
        arrived((z + 4) % NZ, g)
        if g == 0:
            phase("azwait")
            prefix()
        phase(f"dft{g}")
        transform(g)
        phase(f"asend{g}")
        for k in (2, 1, 3):
            a_copy(g, (x + k) % NX).start()
        zrecv[x, g] = zsend[g, :, pl.ds(pl.multiple_of(x * 8 * GROWS, 8 * GROWS), 8 * GROWS), :]

    def b_copy(g, peer):
        return remote(fsend.at[g, peer],
                      landing.at[core, g, :, pl.ds(pl.multiple_of(x * 512, 512), 512)],
                      bsend, brecv.at[g], at_b(peer))

    def combine(g):
        phase(f"await{g}")
        remote(zrecv.at[pl.ds(0, 3), g], zrecv.at[pl.ds(0, 3), g], asend, arecv.at[g],
               at_z(right)).wait_recv()
        phase(f"dft4_{g}")
        turn = jnp.where(iota((8, 128), 0) < GROWS, F32(1.0), F32(-1.0))
        for dc in range(2):
            for ql in range(2):
                for h in range(2):
                    start = (dc * 2 + ql) * 8
                    t = [zrecv[b, g, h, start:start + 8, :] for b in range(NX)]
                    even, odd = t[0] + t[2], t[1] + t[3]
                    differ = t[0] - t[2]
                    turned = pltpu.roll(t[1] - t[3], GROWS, axis=0) * turn
                    results = (even + odd, differ + turned, even - odd, differ - turned)
                    for dx in range(NX):
                        fsend[g, dx * NCORE + dc, :, (ql * 2 + h) * 128:(ql * 2 + h + 1) * 128] = results[dx]

        for peer in partners:
            b_copy(g, peer).start()
        landing[core, g, :, pl.ds(pl.multiple_of(x * 512, 512), 512)] = fsend[g, me]

    def deliver(g):
        phase(f"bwait{g}")

        remote(fsend.at[g, pl.ds(0, 7)], fsend.at[g, pl.ds(0, 7)], bsend, brecv.at[g],
               at_z(right)).wait_recv()
        if g == 0:
            phase("cwait")
            normalization()
        phase(f"out{g}")
        scale = known[2]
        for c in range(NCORE):
            for p in range(2):
                out[p, c * HALF + g * GROWS:c * HALF + (g + 1) * GROWS, :] = (
                    landing[c, g, p * GROWS:(p + 1) * GROWS, :] * scale)

    for _, name, work in sorted(schedule(ring_step, finish, combine, deliver, small_y, small_z),
                                key=lambda e: e[0]):
        phase(name)
        work()

    phase("drain")

    @pl.loop(y + 1, NY)
    def _(k):
        y_copy(k, y).wait_send()

    for ref, semaphore in ((p1s.at[seven, :], p1send), (zslots.at[pl.ds(0, 7)], azsend),
                           (cslots.at[pl.ds(0, 7)], csend), (gathered.at[pl.ds(0, 7)], p2send),
                           (zrecv.at[pl.ds(0, 3)], asend), (fsend.at[:, pl.ds(0, 7)], bsend)):
        remote(ref, ref, semaphore, p1recv, at_z(right)).wait_send()
    phase(None)


def schedule(ring_step, finish, combine, deliver, small_y, small_z):
    hop, lag, fin, exch = PACE
    part = functools.partial
    events = [(SMALL[0], "ysmall", small_y), (SMALL[1], "zsmall", small_z)]
    for g in range(GROUPS):
        for step in range(4):
            events.append((hop * step + lag * g, f"r{step}{g}", part(ring_step, step, g)))
        done = hop * 4 + fin * g
        events.append((done, f"fin{g}", part(finish, g)))
        events.append((done + exch, f"await{g}", part(combine, g)))
        events.append((done + 2 * exch + 10.0, f"bwait{g}", part(deliver, g)))
    return events


PACE = (2.2, 1.0, 1.2, 5.0)
SMALL = (0.5, 3.3)


def per_device(phase_codes, aperture, tile_offsets):
    dma = pltpu.SemaphoreType.DMA
    vmem = pltpu.VMEM
    return pl.pallas_call(
        kernel,
        out_shape=pltpu.VMEM((2, ROWS, 2048), F32),
        in_specs=[pl.BlockSpec(memory_space=pl.ANY)] * 3,
        out_specs=pl.BlockSpec(memory_space=pltpu.VMEM),
        scratch_shapes=[
            vmem((ROWS, 512), I32), vmem((ROWS, 512), I32), vmem((1, 2), I32),
            vmem((NY, NB, 128), F32), vmem((NZ, 16, 128), F32), vmem((NY, NB, 128), F32),
            vmem((NB * MSG, 128), F32), vmem((NB * MSG, 128), F32),
            vmem((NZ, HALF, 16, 128), F32),
            vmem((256, 128), F32), vmem((256, 128), F32),
            vmem((512, 384), BF16), vmem((64, 256), BF16),
            vmem((GROUPS, 2, 32 * GROWS, 128), F32),
            vmem((NX, GROUPS, 2, 8 * GROWS, 128), F32),
            vmem((GROUPS, NB, 2 * GROWS, 512), F32),
            vmem((NCORE, GROUPS, 2 * GROWS, 2048), F32),
            pltpu.SemaphoreType.REGULAR, pltpu.SemaphoreType.REGULAR, dma((3,)),
            dma, dma, dma((NY,)), dma((NY,)), dma, dma, dma, dma,
            dma, dma((NZ, GROUPS)), dma, dma((GROUPS,)), dma, dma((GROUPS,)),
        ],
        compiler_params=pltpu.CompilerParams(collective_id=0, has_side_effects=True),
    )(phase_codes, aperture, tile_offsets.reshape(1, 2))


def solution(mesh):
    placed = (P("row", "col"), P("row", "col"), P("row", "col"))
    return jax.shard_map(
        per_device, mesh=mesh, in_specs=placed, out_specs=P(None, "row", "col"), check_vma=False
    )
```

```python
import functools
import math

import jax
import jax.numpy as jnp
from jax import lax
from jax.experimental import pallas as pl
from jax.experimental.pallas import tpu as pltpu
from jax.sharding import PartitionSpec as P

MESH = pl.DeviceIdType.MESH
F32, I32, BF16 = jnp.float32, jnp.int32, jnp.bfloat16

NY, NX, NZ, NCORE = 8, 4, 8, 2
NB = NX * NCORE
ROWS = 32
HALF = 16
GROUPS = 4
GROWS = HALF // GROUPS


def cos_sin(index, bits):
    size = 1 << bits
    index = index & (size - 1)
    quadrant = (index + (size >> 3)) >> (bits - 2)
    rest = index - (quadrant << (bits - 2))
    x = rest.astype(F32) * F32(2.0 * math.pi / size)
    y = x * x
    s = x * (1.0 + y * (-1.0 / 6 + y * (1.0 / 120 + y * (-1.0 / 5040 + y * (1.0 / 362880)))))
    c = 1.0 + y * (-0.5 + y * (1.0 / 24 + y * (-1.0 / 720 + y * (1.0 / 40320))))
    quadrant = quadrant & 3
    swap = (quadrant & 1) == 1
    cos = jnp.where(swap, s, c)
    sin = jnp.where(swap, c, s)
    cos = jnp.where((quadrant == 1) | (quadrant == 2), -cos, cos)
    sin = jnp.where(quadrant >= 2, -sin, sin)
    return cos, sin


def halves(value):
    high = value.astype(BF16)
    return high, (value - high.astype(F32)).astype(BF16)


def iota(shape, axis):
    return lax.broadcasted_iota(I32, shape, axis)


def rotation(cos, sin, part_out, part_in):
    cross = jnp.where(part_out == 0, sin, -sin)
    return jnp.where(part_out == part_in, cos, cross)


def phase(name):
    pass


def kernel(codes_in, aperture_in, offsets_in, out, codes, aperture, offsets, xslots, yslots, zslots, cslots,
           p1s, p1r, gathered, tcos, tsin, wmat, emat, zsend, zrecv, fsend, landing,
           ready_y, ready_z, insem, p1send, p1recv, xsend, xrecv, ysend, yrecv, azsend, azrecv, csend, crecv,
           p2send, p2recv, asend, arecv, bsend, brecv):
    y = lax.axis_index("row")
    col = lax.axis_index("col")
    core = col % NCORE
    z = (col // NCORE) % NZ
    x = col // (NCORE * NZ)
    me = x * NCORE + core

    def at_y(k):
        return (k, col)

    def at_b(k):
        return (y, ((k // NCORE) * NZ + z) * NCORE + k % NCORE)

    def at_z(k):
        return (y, (x * NZ + k) * NCORE + core)

    def remote(src, dst, ss, rs, where):
        return pltpu.make_async_remote_copy(
            src_ref=src, dst_ref=dst, send_sem=ss, recv_sem=rs,
            device_id=where, device_id_type=MESH)

    phase("start")
    barrier = pltpu.get_barrier_semaphore()

    def signal(semaphore, where):
        pl.semaphore_signal(semaphore, inc=1, device_id=where, device_id_type=MESH)

    partners = [((x + dx) % NX) * NCORE + (core + dc) % NCORE
                for dx, dc in ((2, 0), (2, 1), (1, 0), (3, 0), (1, 1), (3, 1), (0, 1))]
    right, left = (z + 1) % NZ, (z + NZ - 1) % NZ
    for peer in partners:
        signal(barrier, at_b(peer))
    for peer in (right, left):
        signal(barrier, at_z(peer))
    for k in range(2, NZ - 1):
        peer = (z + k) % NZ

        @pl.when(peer > z)
        def _():
            signal(barrier, at_z(peer))

    @pl.loop(y + 1, NY)
    def _(k):
        signal(barrier, at_y(k))

    loads = [pltpu.make_async_copy(codes_in, codes, insem.at[0]),
             pltpu.make_async_copy(aperture_in, aperture, insem.at[1]),
             pltpu.make_async_copy(offsets_in, offsets, insem.at[2])]
    for load in loads:
        load.start()
    i, j = iota((512, 512), 0), iota((512, 512), 1)
    pick = jnp.where(i == 4 * (j & 127) + (j >> 7), 1.0, 0.0).astype(BF16)
    for load in loads:
        load.wait()

    phase("field")
    off0, off1 = offsets[:, 0:1], offsets[:, 1:2]
    opened = aperture[...]
    per_lane = jnp.sum(opened, axis=0, keepdims=True)
    count = sum(per_lane[:, j * 128:(j + 1) * 128] for j in range(4))
    total = jnp.broadcast_to(off0 + off1, (1, 128)).astype(F32)
    count = count.astype(F32)

    row = iota((ROWS, 512), 0)
    code = codes[...] + jnp.where(row < 16, off0, off0 + off1)
    code = code & 4095
    marked = jnp.concatenate([(code >> 6) + 64 * opened, code & 63], axis=0)
    moved = jnp.dot(marked.astype(F32).astype(BF16), pick, preferred_element_type=F32)
    moved = moved.astype(I32)
    high, low = moved[:ROWS], moved[ROWS:]
    amplitude = (high >> 6).astype(F32)
    cos, sin = cos_sin(((high & 63) << 6) + low, 12)
    field = (amplitude * cos, amplitude * sin)
    for b in range(NB):
        bx, bc = b // NCORE, b % NCORE
        for part in range(2):
            for g in range(GROUPS):
                first = bc * HALF + g * GROWS
                p1s[g, b * 8 + part * GROWS:b * 8 + (part + 1) * GROWS, :] = (
                    field[part][first:first + GROWS, bx * 128:(bx + 1) * 128])
    xslots[me, 0:1, :] = total
    xslots[me, 1:2, :] = count

    phase("barrier")
    entered_z = z - (z + 6) // 7 - z // 7
    pl.semaphore_wait(barrier, 9 + entered_z + y)

    phase("startp1")

    def p1_copy(g, peer):
        return remote(p1s.at[g, pl.ds(pl.multiple_of(peer * 8, 8), 8), :],
                      p1r.at[g, pl.ds(pl.multiple_of(me * 8, 8), 8), :],
                      p1send, p1recv.at[g], at_b(peer))

    for peer in partners:
        p1_copy(0, peer).start()
    for peer in partners:
        remote(xslots.at[me], xslots.at[me], xsend, xrecv, at_b(peer)).start()
    for g in range(1, GROUPS):
        for peer in partners:
            p1_copy(g, peer).start()
    for k in range(2, NZ - 1):
        peer = (z + k) % NZ

        @pl.when(peer < z)
        def _():
            signal(ready_z, at_z(peer))

    @pl.loop(0, y)
    def _(k):
        signal(ready_y, at_y(k))

    own = pl.ds(pl.multiple_of(me * 8, 8), 8)
    for g in range(GROUPS):
        p1r[g, own, :] = p1s[g, own, :]

    phase("tables")
    shape = (512, 128)
    i, j = iota(shape, 0), iota(shape, 1)
    source = j & 7
    a = ((source >> 1) * NZ + ((j >> 3) & 7)) * NCORE + (source & 1)
    cos, sin = cos_sin(a * (i & 255), 8)
    w_high, w_low = halves(rotation(cos, sin, i >> 8, j >> 6))
    wmat[:, 0:128] = w_high
    wmat[:, 128:256] = w_high
    wmat[:, 256:384] = w_low
    shape = (256, 128)
    cos, sin = cos_sin((4 * iota(shape, 1) + x) * iota(shape, 0), 17)
    tcos[...] = cos
    tsin[...] = sin
    shape = (32, 256)
    i, j = iota(shape, 0), iota(shape, 1)
    q = 2 * (i >> 3) + ((i >> 1) & 1)
    d_low = NCORE * z + ((i >> 2) & 1)
    cos, sin = cos_sin((4 * (j & 127) + x) * (8 * d_low + q), 9)
    e_high, e_low = halves(rotation(cos, sin, i & 1, j >> 7))
    emat[0:32, :] = e_high
    emat[32:64, :] = e_low

    def receive(g):
        messages = p1r.at[g, pl.ds(0, 56), :]
        remote(messages, messages, p1send, p1recv.at[g], at_z(right)).wait_recv()
        for n in range(GROWS):
            for part in range(2):
                gathered[z, g * GROWS + n, part * 8:(part + 1) * 8, :] = (
                    p1r[g, pl.ds(part * GROWS + n, NB, stride=8), :])

    def ring(block, group, way, step):
        part = gathered.at[block, pl.ds(group * GROWS, GROWS)]
        return remote(part, part, p2send, p2recv.at[block, group],
                      at_z(right if way == 0 else left))

    def ring_block(way, step):
        return (z + NZ - step) % NZ if way == 0 else (z + step) % NZ

    def forwards(way, step, group):
        return step < 3 or (group % 2 == 0) == (way == 0)

    def arrived(block, group):
        part = gathered.at[block, pl.ds(group * GROWS, GROWS)]
        remote(part, part, p2send, p2recv.at[block, group],
               at_z(left)).wait_recv()

    def ring_step(step, group):
        if step == 0:
            receive(group)
        for way in range(2):
            if step:
                arrived(ring_block(way, step), group)
            if forwards(way, step, group):
                ring(ring_block(way, step), group, way, step).start()

    def y_copy(peer, slot):
        return remote(yslots.at[slot], yslots.at[slot], ysend.at[peer], yrecv.at[slot], at_y(peer))

    def az_copy(peer):
        return remote(zslots.at[z], zslots.at[z], azsend, azrecv, at_z(peer))

    def c_copy(peer):
        return remote(cslots.at[y], cslots.at[y], csend, crecv, at_y(peer))

    def small_y():
        remote(xslots.at[pl.ds(0, 7)], xslots.at[pl.ds(0, 7)], xsend, xrecv, at_z(right)).wait_recv()
        yslots[y] = xslots[:, 0, :]
        @pl.when(y < NY - 1)
        def _():
            pl.semaphore_wait(ready_y, NY - 1 - y)

        @pl.loop(y + 1, NY)
        def _(k):
            y_copy(k, y).start()

    def small_z():
        @pl.loop(0, y)
        def _(k):
            y_copy(k, k).wait_recv()
        before = lax.fori_loop(0, y, lambda k, acc: acc + yslots[k], jnp.zeros((NB, 128), F32))
        zslots[z, 0:8, :] = before
        zslots[z, 8:16, :] = xslots[:, 1, :]
        @pl.when(z < NZ - 2)
        def _():
            pl.semaphore_wait(ready_z, 5 + (z + 6) // 7 - z)

        @pl.loop(1, NZ)
        def _(k):
            az_copy((z + k) % NZ).start()

    known = []

    def prefix():
        remote(zslots.at[pl.ds(0, 7)], zslots.at[pl.ds(0, 7)], azsend, azrecv, at_z(right)).wait_recv()
        known.extend(cos_sin(zslots[:, 0:8, :].astype(I32), 12))
        cslots[y] = jnp.sum(zslots[:, 8:16, :], axis=0)

        @pl.loop(1, NY)
        def _(k):
            c_copy((y + k) % NY).start()

    def normalization():
        remote(cslots.at[pl.ds(0, 7)], cslots.at[pl.ds(0, 7)], csend, crecv, at_z(right)).wait_recv()
        total = jnp.sum(cslots[...], axis=0)
        total = jnp.sum(jnp.sum(total, axis=0, keepdims=True), axis=1, keepdims=True)
        known.append(jnp.sqrt(F32(ROWS * NY) / total))

    nt = (((1,), (1,)), ((), ()))

    def a_copy(g, peer):
        return remote(zsend.at[g, :, pl.ds(peer * 8 * GROWS, 8 * GROWS), :], zrecv.at[x, g],
                      asend, arecv.at[g], at_b(peer * NCORE + core))

    def transform(g):
        pcos, psin = known[:2]
        for pair in range(GROWS // 2):
            columns = []
            for n in range(2):
                block = gathered[:, g * GROWS + pair * 2 + n]
                re, im = block[:, 0:8, :], block[:, 8:16, :]
                columns.append(jnp.concatenate(
                    [(re * pcos - im * psin).reshape(64, 128),
                     (re * psin + im * pcos).reshape(64, 128)], axis=0))
            high, low = halves(jnp.concatenate(columns, axis=1))
            spec = jnp.dot(wmat[...], jnp.concatenate([high, low, high], axis=0),
                           preferred_element_type=F32)
            for n in range(2):
                re = spec[0:256, n * 128:(n + 1) * 128]
                im = spec[256:512, n * 128:(n + 1) * 128]
                c, s = tcos[...], tsin[...]
                turned = jnp.concatenate([re * c + im * s, im * c - re * s], axis=1)
                high, low = halves(turned)
                first = lax.dot_general(emat[...], high, nt, preferred_element_type=F32)
                second = lax.dot_general(emat[0:32, :], low, nt, preferred_element_type=F32)
                result = first[0:32] + first[32:64] + second
                for h in range(2):
                    zsend[g, h, pl.ds(pair * 2 + n, 32, stride=GROWS), :] = (
                        result[:, h * 128:(h + 1) * 128])

    def finish(g):
        phase(f"fin{g}")
        arrived((z + 4) % NZ, g)
        if g == 0:
            phase("azwait")
            prefix()
        phase(f"dft{g}")
        transform(g)
        phase(f"asend{g}")
        for k in (2, 1, 3):
            a_copy(g, (x + k) % NX).start()
        zrecv[x, g] = zsend[g, :, pl.ds(pl.multiple_of(x * 8 * GROWS, 8 * GROWS), 8 * GROWS), :]

    def b_copy(g, peer):
        return remote(fsend.at[g, peer],
                      landing.at[core, g, :, pl.ds(pl.multiple_of(x * 512, 512), 512)],
                      bsend, brecv.at[g], at_b(peer))

    def combine(g):
        phase(f"await{g}")
        remote(zrecv.at[pl.ds(0, 3), g], zrecv.at[pl.ds(0, 3), g], asend, arecv.at[g],
               at_z(right)).wait_recv()
        phase(f"dft4_{g}")
        turn = jnp.where(iota((8, 128), 0) < GROWS, F32(1.0), F32(-1.0))
        for dc in range(2):
            for ql in range(2):
                for h in range(2):
                    start = (dc * 2 + ql) * 8
                    t = [zrecv[b, g, h, start:start + 8, :] for b in range(NX)]
                    even, odd = t[0] + t[2], t[1] + t[3]
                    differ = t[0] - t[2]
                    turned = pltpu.roll(t[1] - t[3], GROWS, axis=0) * turn
                    results = (even + odd, differ + turned, even - odd, differ - turned)
                    for dx in range(NX):
                        fsend[g, dx * NCORE + dc, :, (ql * 2 + h) * 128:(ql * 2 + h + 1) * 128] = results[dx]

        for peer in partners:
            b_copy(g, peer).start()
        landing[core, g, :, pl.ds(pl.multiple_of(x * 512, 512), 512)] = fsend[g, me]

    def deliver(g):
        phase(f"bwait{g}")

        remote(fsend.at[g, pl.ds(0, 7)], fsend.at[g, pl.ds(0, 7)], bsend, brecv.at[g],
               at_z(right)).wait_recv()
        if g == 0:
            phase("cwait")
            normalization()
        phase(f"out{g}")
        scale = known[2]
        for c in range(NCORE):
            for p in range(2):
                out[p, c * HALF + g * GROWS:c * HALF + (g + 1) * GROWS, :] = (
                    landing[c, g, p * GROWS:(p + 1) * GROWS, :] * scale)

    for _, name, work in sorted(schedule(ring_step, finish, combine, deliver, small_y, small_z),
                                key=lambda e: e[0]):
        phase(name)
        work()

    phase("drain")

    @pl.loop(y + 1, NY)
    def _(k):
        y_copy(k, y).wait_send()

    for ref, semaphore in ((p1s.at[:, pl.ds(0, 56), :], p1send), (xslots.at[pl.ds(0, 7)], xsend),
                           (zslots.at[pl.ds(0, 7)], azsend),
                           (cslots.at[pl.ds(0, 7)], csend), (gathered.at[pl.ds(0, 7)], p2send),
                           (zrecv.at[pl.ds(0, 3)], asend), (fsend.at[:, pl.ds(0, 7)], bsend)):
        remote(ref, ref, semaphore, xrecv, at_z(right)).wait_send()
    phase(None)


def schedule(ring_step, finish, combine, deliver, small_y, small_z):
    part = functools.partial
    events = [(SMALL[0], "ysmall", small_y), (SMALL[1], "zsmall", small_z)]
    for g in range(GROUPS):
        for step in range(4):
            events.append((RING[step] + g * LAG, f"r{step}{g}", part(ring_step, step, g)))
    for g in range(GROUPS):
        events.append((FIN[g], f"fin{g}", part(finish, g)))
        events.append((FOUR[g], f"await{g}", part(combine, g)))
        events.append((100.0 + g, f"bwait{g}", part(deliver, g)))
    return events


RING = (0.0, 2.2, 4.4, 6.6)
LAG = 1.0
SMALL = (2.3, 6.0)
FIN = (8.8, 10.0, 11.2, 12.4)
FOUR = (13.5, 15.0, 16.5, 18.0)


def per_device(phase_codes, aperture, tile_offsets):
    dma = pltpu.SemaphoreType.DMA
    vmem = pltpu.VMEM
    return pl.pallas_call(
        kernel,
        out_shape=pltpu.VMEM((2, ROWS, 2048), F32),
        in_specs=[pl.BlockSpec(memory_space=pl.ANY)] * 3,
        out_specs=pl.BlockSpec(memory_space=pltpu.VMEM),
        scratch_shapes=[
            vmem((ROWS, 512), I32), vmem((ROWS, 512), I32), vmem((1, 2), I32),
            vmem((NB, 2, 128), F32), vmem((NY, NB, 128), F32), vmem((NZ, 16, 128), F32), vmem((NY, NB, 128), F32),
            vmem((GROUPS, NB * 8, 128), F32), vmem((GROUPS, NB * 8, 128), F32),
            vmem((NZ, HALF, 16, 128), F32),
            vmem((256, 128), F32), vmem((256, 128), F32),
            vmem((512, 384), BF16), vmem((64, 256), BF16),
            vmem((GROUPS, 2, 32 * GROWS, 128), F32),
            vmem((NX, GROUPS, 2, 8 * GROWS, 128), F32),
            vmem((GROUPS, NB, 2 * GROWS, 512), F32),
            vmem((NCORE, GROUPS, 2 * GROWS, 2048), F32),
            pltpu.SemaphoreType.REGULAR, pltpu.SemaphoreType.REGULAR, dma((3,)),
            dma, dma((GROUPS,)), dma, dma, dma((NY,)), dma((NY,)), dma, dma, dma, dma,
            dma, dma((NZ, GROUPS)), dma, dma((GROUPS,)), dma, dma((GROUPS,)),
        ],
        compiler_params=pltpu.CompilerParams(collective_id=0, has_side_effects=True),
    )(phase_codes, aperture, tile_offsets.reshape(1, 2))


def solution(mesh):
    placed = (P("row", "col"), P("row", "col"), P("row", "col"))
    return jax.shard_map(
        per_device, mesh=mesh, in_specs=placed, out_specs=P(None, "row", "col"), check_vma=False
    )
```

```python
import functools
import math

import jax
import jax.numpy as jnp
from jax import lax
from jax.experimental import pallas as pl
from jax.experimental.pallas import tpu as pltpu
from jax.sharding import PartitionSpec as P

MESH = pl.DeviceIdType.MESH
F32, I32, BF16 = jnp.float32, jnp.int32, jnp.bfloat16

NY, NX, NZ, NCORE = 8, 4, 8, 2
NB = NX * NCORE
ROWS = 32
HALF = 16
GROUPS = 4
GROWS = HALF // GROUPS


def cos_sin(index, bits):
    size = 1 << bits
    index = index & (size - 1)
    quadrant = (index + (size >> 3)) >> (bits - 2)
    rest = index - (quadrant << (bits - 2))
    x = rest.astype(F32) * F32(2.0 * math.pi / size)
    y = x * x
    s = x * (1.0 + y * (-1.0 / 6 + y * (1.0 / 120 + y * (-1.0 / 5040 + y * (1.0 / 362880)))))
    c = 1.0 + y * (-0.5 + y * (1.0 / 24 + y * (-1.0 / 720 + y * (1.0 / 40320))))
    quadrant = quadrant & 3
    swap = (quadrant & 1) == 1
    cos = jnp.where(swap, s, c)
    sin = jnp.where(swap, c, s)
    cos = jnp.where((quadrant == 1) | (quadrant == 2), -cos, cos)
    sin = jnp.where(quadrant >= 2, -sin, sin)
    return cos, sin


def halves(value):
    high = value.astype(BF16)
    return high, (value - high.astype(F32)).astype(BF16)


def iota(shape, axis):
    return lax.broadcasted_iota(I32, shape, axis)


def rotation(cos, sin, part_out, part_in):
    cross = jnp.where(part_out == 0, sin, -sin)
    return jnp.where(part_out == part_in, cos, cross)


def phase(name):
    pass


def kernel(codes_in, aperture_in, offsets_in, out, codes, aperture, offsets, xslots, yslots, zslots, cslots,
           p1s, p1r, gathered, tcos, tsin, wmat, emat, zsend, zrecv, fsend, landing,
           ready_y, ready_z, insem, p1send, p1recv, xsend, xrecv, ysend, yrecv, azsend, azrecv, csend, crecv,
           p2send, p2recv, asend, arecv, bsend, brecv):
    y = lax.axis_index("row")
    col = lax.axis_index("col")
    core = col % NCORE
    z = (col // NCORE) % NZ
    x = col // (NCORE * NZ)
    me = x * NCORE + core

    def at_y(k):
        return (k, col)

    def at_b(k):
        return (y, ((k // NCORE) * NZ + z) * NCORE + k % NCORE)

    def at_z(k):
        return (y, (x * NZ + k) * NCORE + core)

    def remote(src, dst, ss, rs, where):
        return pltpu.make_async_remote_copy(
            src_ref=src, dst_ref=dst, send_sem=ss, recv_sem=rs,
            device_id=where, device_id_type=MESH)

    phase("start")
    barrier = pltpu.get_barrier_semaphore()

    def signal(semaphore, where):
        pl.semaphore_signal(semaphore, inc=1, device_id=where, device_id_type=MESH)

    partners = [((x + dx) % NX) * NCORE + (core + dc) % NCORE
                for dx, dc in ((2, 0), (2, 1), (1, 0), (3, 0), (1, 1), (3, 1), (0, 1))]
    right, left = (z + 1) % NZ, (z + NZ - 1) % NZ
    for peer in partners:
        signal(barrier, at_b(peer))
    for peer in (right, left):
        signal(barrier, at_z(peer))
    for k in range(2, NZ - 1):
        peer = (z + k) % NZ

        @pl.when(peer > z)
        def _():
            signal(barrier, at_z(peer))

    @pl.loop(y + 1, NY)
    def _(k):
        signal(barrier, at_y(k))

    loads = [pltpu.make_async_copy(codes_in, codes, insem.at[0]),
             pltpu.make_async_copy(aperture_in, aperture, insem.at[1]),
             pltpu.make_async_copy(offsets_in, offsets, insem.at[2])]
    for load in loads:
        load.start()
    i, j = iota((512, 512), 0), iota((512, 512), 1)
    pick = jnp.where(i == 4 * (j & 127) + (j >> 7), 1.0, 0.0).astype(BF16)
    for load in loads:
        load.wait()

    phase("field")
    off0, off1 = offsets[:, 0:1], offsets[:, 1:2]
    opened = aperture[...]
    per_lane = jnp.sum(opened, axis=0, keepdims=True)
    count = sum(per_lane[:, j * 128:(j + 1) * 128] for j in range(4))
    total = jnp.broadcast_to(off0 + off1, (1, 128)).astype(F32)
    count = count.astype(F32)

    row = iota((ROWS, 512), 0)
    code = codes[...] + jnp.where(row < 16, off0, off0 + off1)
    code = code & 4095
    marked = jnp.concatenate([(code >> 6) + 64 * opened, code & 63], axis=0)
    moved = jnp.dot(marked.astype(F32).astype(BF16), pick, preferred_element_type=F32)
    moved = moved.astype(I32)
    high, low = moved[:ROWS], moved[ROWS:]
    amplitude = (high >> 6).astype(F32)
    cos, sin = cos_sin(((high & 63) << 6) + low, 12)
    field = (amplitude * cos, amplitude * sin)
    for b in range(NB):
        bx, bc = b // NCORE, b % NCORE
        for part in range(2):
            for g in range(GROUPS):
                first = bc * HALF + g * GROWS
                p1s[g, b * 8 + part * GROWS:b * 8 + (part + 1) * GROWS, :] = (
                    field[part][first:first + GROWS, bx * 128:(bx + 1) * 128])
    xslots[me, 0:1, :] = total
    xslots[me, 1:2, :] = count

    phase("barrier")
    entered_z = z - (z + 6) // 7 - z // 7
    pl.semaphore_wait(barrier, 9 + entered_z + y)

    phase("startp1")

    def p1_copy(g, peer):
        return remote(p1s.at[g, pl.ds(pl.multiple_of(peer * 8, 8), 8), :],
                      p1r.at[g, pl.ds(pl.multiple_of(me * 8, 8), 8), :],
                      p1send, p1recv.at[g], at_b(peer))

    for peer in partners:
        p1_copy(0, peer).start()
    for peer in partners:
        remote(xslots.at[me], xslots.at[me], xsend, xrecv, at_b(peer)).start()
    for g in range(1, GROUPS):
        for peer in partners:
            p1_copy(g, peer).start()
    for k in range(2, NZ - 1):
        peer = (z + k) % NZ

        @pl.when(peer < z)
        def _():
            signal(ready_z, at_z(peer))

    @pl.loop(0, y)
    def _(k):
        signal(ready_y, at_y(k))

    own = pl.ds(pl.multiple_of(me * 8, 8), 8)
    for g in range(GROUPS):
        p1r[g, own, :] = p1s[g, own, :]

    phase("tables")
    shape = (256, 192)
    i, j = iota(shape, 0), iota(shape, 1)
    for c in range(NCORE):
        a = ((j & 3) * NZ + ((j >> 3) & 7)) * NCORE + c
        cos, sin = cos_sin(a * (i & 127), 8)
        weight = rotation(cos, sin, i >> 7, (j >> 2) & 1)
        high = weight.astype(BF16).astype(F32)
        wmat[c] = jnp.where(j < 128, high, weight - high).astype(BF16)
    shape = (256, 128)
    cos, sin = cos_sin((4 * iota(shape, 1) + x) * iota(shape, 0), 17)
    tcos[...] = cos
    tsin[...] = sin
    shape = (32, 256)
    i, j = iota(shape, 0), iota(shape, 1)
    q = 2 * (i >> 3) + ((i >> 1) & 1)
    d_low = NCORE * z + ((i >> 2) & 1)
    cos, sin = cos_sin((4 * (j & 127) + x) * (8 * d_low + q), 9)
    e_high, e_low = halves(rotation(cos, sin, i & 1, j >> 7))
    emat[0:32, :] = e_high
    emat[32:64, :] = e_low

    def receive(g):
        messages = p1r.at[g, pl.ds(0, 56), :]
        remote(messages, messages, p1send, p1recv.at[g], at_z(right)).wait_recv()
        for n in range(GROWS):
            for c in range(NCORE):
                for part in range(2):
                    spot = c * 8 + part * NX
                    gathered[z, g * GROWS + n, spot:spot + NX, :] = (
                        p1r[g, pl.ds(c * 8 + part * GROWS + n, NX, stride=8 * NCORE), :])

    def ring(block, group, way, step):
        part = gathered.at[block, pl.ds(group * GROWS, GROWS)]
        return remote(part, part, p2send, p2recv.at[block, group],
                      at_z(right if way == 0 else left))

    def ring_block(way, step):
        return (z + NZ - step) % NZ if way == 0 else (z + step) % NZ

    def forwards(way, step, group):
        return step < 3 or (group % 2 == 0) == (way == 0)

    def arrived(block, group):
        part = gathered.at[block, pl.ds(group * GROWS, GROWS)]
        remote(part, part, p2send, p2recv.at[block, group],
               at_z(left)).wait_recv()

    def ring_step(step, group):
        if step == 0:
            receive(group)
        for way in range(2):
            if step:
                arrived(ring_block(way, step), group)
            if forwards(way, step, group):
                ring(ring_block(way, step), group, way, step).start()

    def y_copy(peer, slot):
        return remote(yslots.at[slot], yslots.at[slot], ysend.at[peer], yrecv.at[slot], at_y(peer))

    def az_copy(peer):
        return remote(zslots.at[z], zslots.at[z], azsend, azrecv, at_z(peer))

    def c_copy(peer):
        return remote(cslots.at[y], cslots.at[y], csend, crecv, at_y(peer))

    def small_y():
        remote(xslots.at[pl.ds(0, 7)], xslots.at[pl.ds(0, 7)], xsend, xrecv, at_z(right)).wait_recv()
        for k in range(NB):
            yslots[y, k:k + 1, :] = xslots[k % NX * NCORE + k // NX, 0:1, :]
        @pl.when(y < NY - 1)
        def _():
            pl.semaphore_wait(ready_y, NY - 1 - y)

        @pl.loop(y + 1, NY)
        def _(k):
            y_copy(k, y).start()

    def small_z():
        @pl.loop(0, y)
        def _(k):
            y_copy(k, k).wait_recv()
        before = lax.fori_loop(0, y, lambda k, acc: acc + yslots[k], jnp.zeros((NB, 128), F32))
        shape = (NB, 128)
        diagonal = jnp.where(iota(shape, 0) == (iota(shape, 1) & 7), before, 0.0)
        zslots[z, 0:1, :] = jnp.sum(diagonal, axis=0, keepdims=True)
        zslots[z, 1:2, :] = jnp.sum(xslots[:, 1, :], axis=0, keepdims=True)
        @pl.when(z < NZ - 2)
        def _():
            pl.semaphore_wait(ready_z, 5 + (z + 6) // 7 - z)

        @pl.loop(1, NZ)
        def _(k):
            az_copy((z + k) % NZ).start()

    known = []

    def prefix():
        remote(zslots.at[pl.ds(0, 7)], zslots.at[pl.ds(0, 7)], azsend, azrecv, at_z(right)).wait_recv()
        shape = (NZ, 8, 128)
        sublane, lane = iota(shape, 1), iota(shape, 2)
        sign = jnp.where(sublane < NX, F32(-1.0), F32(1.0))
        every = jnp.broadcast_to(zslots[:, 0:1, :], shape)
        turns = []
        for c in range(NCORE):
            mine = jnp.where(lane == c * NX + (sublane & 3), every, 0.0)
            before = jnp.broadcast_to(jnp.sum(mine, axis=2, keepdims=True), shape)
            cos, sin = cos_sin(before.astype(I32), 12)
            turns.append((cos, sin * sign))
        known.append(turns)
        cslots[y] = zslots[:, 1, :]

        @pl.loop(1, NY)
        def _(k):
            c_copy((y + k) % NY).start()

    def normalization():
        remote(cslots.at[pl.ds(0, 7)], cslots.at[pl.ds(0, 7)], csend, crecv, at_z(right)).wait_recv()
        total = jnp.sum(cslots[...], axis=0)
        total = jnp.sum(jnp.sum(total, axis=0, keepdims=True), axis=1, keepdims=True)
        known.append(jnp.sqrt(F32(ROWS * NY) / total))

    nt = (((1,), (1,)), ((), ()))

    def a_copy(g, peer):
        return remote(zsend.at[g, :, pl.ds(peer * 8 * GROWS, 8 * GROWS), :], zrecv.at[x, g],
                      asend, arecv.at[g], at_b(peer * NCORE + core))

    def transform(g):
        for pair in range(GROWS // 2):
            parity = []
            for c in range(NCORE):
                cos, sin = known[0][c]
                columns = []
                for n in range(2):
                    block = gathered[:, g * GROWS + pair * 2 + n, c * 8:(c + 1) * 8, :]
                    columns.append((block * cos + pltpu.roll(block, NX, axis=1) * sin).reshape(64, 128))
                high, low = halves(jnp.concatenate(columns, axis=1))
                parity.append(jnp.dot(wmat[c], jnp.concatenate([high, low, high], axis=0),
                                      preferred_element_type=F32))
            for h, spec in enumerate((parity[0] + parity[1], parity[0] - parity[1])):
                c, s = tcos[h * 128:(h + 1) * 128, :], tsin[h * 128:(h + 1) * 128, :]
                for n in range(2):
                    re = spec[0:128, n * 128:(n + 1) * 128]
                    im = spec[128:256, n * 128:(n + 1) * 128]
                    turned = jnp.concatenate([re * c + im * s, im * c - re * s], axis=1)
                    high, low = halves(turned)
                    first = lax.dot_general(emat[...], high, nt, preferred_element_type=F32)
                    second = lax.dot_general(emat[0:32, :], low, nt, preferred_element_type=F32)
                    zsend[g, h, pl.ds(pair * 2 + n, 32, stride=GROWS), :] = (
                        first[0:32] + first[32:64] + second)

    def finish(first, last):
        if first == 0:
            prefix()

        @pl.loop(first, last)
        def _(g):
            arrived((z + 4) % NZ, g)
            transform(g)
            for k in (2, 1, 3):
                a_copy(g, (x + k) % NX).start()
            zrecv[x, g] = zsend[g, :, pl.ds(pl.multiple_of(x * 8 * GROWS, 8 * GROWS), 8 * GROWS), :]

    def b_copy(g, peer):
        return remote(fsend.at[g, peer],
                      landing.at[core, g, :, pl.ds(pl.multiple_of(x * 512, 512), 512)],
                      bsend, brecv.at[g], at_b(peer))

    def combine(g):
        remote(zrecv.at[pl.ds(0, 3), g], zrecv.at[pl.ds(0, 3), g], asend, arecv.at[g],
               at_z(right)).wait_recv()
        turn = jnp.where(iota((8, 128), 0) < GROWS, F32(1.0), F32(-1.0))
        for dc in range(2):
            for ql in range(2):
                for h in range(2):
                    start = (dc * 2 + ql) * 8
                    t = [zrecv[b, g, h, start:start + 8, :] for b in range(NX)]
                    even, odd = t[0] + t[2], t[1] + t[3]
                    differ = t[0] - t[2]
                    turned = pltpu.roll(t[1] - t[3], GROWS, axis=0) * turn
                    results = (even + odd, differ + turned, even - odd, differ - turned)
                    for dx in range(NX):
                        fsend[g, dx * NCORE + dc, :, (ql * 2 + h) * 128:(ql * 2 + h + 1) * 128] = results[dx]

        for peer in partners:
            b_copy(g, peer).start()
        landing[core, g, :, pl.ds(pl.multiple_of(x * 512, 512), 512)] = fsend[g, me]

    def deliver(g):
        remote(fsend.at[g, pl.ds(0, 7)], fsend.at[g, pl.ds(0, 7)], bsend, brecv.at[g],
               at_z(right)).wait_recv()
        scale = known[1]
        for c in range(NCORE):
            for p in range(2):
                out[p, pl.ds(c * HALF + g * GROWS, GROWS), :] = (
                    landing[c, g, p * GROWS:(p + 1) * GROWS, :] * scale)

    for _, name, work in sorted(schedule(ring_step, finish, small_y, small_z), key=lambda e: e[0]):
        phase(name)
        work()

    phase("combine")
    pl.loop(0, GROUPS)(combine)
    phase("cwait")
    normalization()
    phase("deliver")
    if LOOP_OUT:
        pl.loop(0, GROUPS)(deliver)
    else:
        for g in range(GROUPS):
            deliver(g)

    phase("drain")

    @pl.loop(y + 1, NY)
    def _(k):
        y_copy(k, y).wait_send()

    for ref, semaphore in ((p1s.at[:, pl.ds(0, 56), :], p1send), (xslots.at[pl.ds(0, 7)], xsend),
                           (zslots.at[pl.ds(0, 7)], azsend),
                           (cslots.at[pl.ds(0, 7)], csend), (gathered.at[pl.ds(0, 7)], p2send),
                           (zrecv.at[pl.ds(0, 3)], asend), (fsend.at[:, pl.ds(0, 7)], bsend)):
        remote(ref, ref, semaphore, xrecv, at_z(right)).wait_send()
    phase(None)


def schedule(ring_step, finish, small_y, small_z):
    part = functools.partial
    events = [(SMALL[0], "ysmall", small_y), (SMALL[1], "zsmall", small_z)]
    for g in range(GROUPS):
        for step in range(4):
            events.append((RING[step] + g * LAG, f"r{step}{g}", part(ring_step, step, g)))
    for k in range(len(FIN)):
        first, when = FIN[k]
        last = FIN[k + 1][0] if k + 1 < len(FIN) else GROUPS
        events.append((when, f"fin{first}", part(finish, first, last)))
    return events


RING = (0.0, 2.2, 4.4, 6.6)
LAG = 1.0
SMALL = (2.3, 6.0)
FIN = ((0, 8.8), (1, 10.0))
LOOP_OUT = False


def per_device(phase_codes, aperture, tile_offsets):
    dma = pltpu.SemaphoreType.DMA
    vmem = pltpu.VMEM
    return pl.pallas_call(
        kernel,
        out_shape=pltpu.VMEM((2, ROWS, 2048), F32),
        in_specs=[pl.BlockSpec(memory_space=pl.ANY)] * 3,
        out_specs=pl.BlockSpec(memory_space=pltpu.VMEM),
        scratch_shapes=[
            vmem((ROWS, 512), I32), vmem((ROWS, 512), I32), vmem((1, 2), I32),
            vmem((NB, 2, 128), F32), vmem((NY, NB, 128), F32), vmem((NZ, 2, 128), F32), vmem((NY, NB, 128), F32),
            vmem((GROUPS, NB * 8, 128), F32), vmem((GROUPS, NB * 8, 128), F32),
            vmem((NZ, HALF, 16, 128), F32),
            vmem((256, 128), F32), vmem((256, 128), F32),
            vmem((NCORE, 256, 192), BF16), vmem((64, 256), BF16),
            vmem((GROUPS, 2, 32 * GROWS, 128), F32),
            vmem((NX, GROUPS, 2, 8 * GROWS, 128), F32),
            vmem((GROUPS, NB, 2 * GROWS, 512), F32),
            vmem((NCORE, GROUPS, 2 * GROWS, 2048), F32),
            pltpu.SemaphoreType.REGULAR, pltpu.SemaphoreType.REGULAR, dma((3,)),
            dma, dma((GROUPS,)), dma, dma, dma((NY,)), dma((NY,)), dma, dma, dma, dma,
            dma, dma((NZ, GROUPS)), dma, dma((GROUPS,)), dma, dma((GROUPS,)),
        ],
        compiler_params=pltpu.CompilerParams(collective_id=0, has_side_effects=True),
    )(phase_codes, aperture, tile_offsets.reshape(1, 2))


def solution(mesh):
    placed = (P("row", "col"), P("row", "col"), P("row", "col"))
    return jax.shard_map(
        per_device, mesh=mesh, in_specs=placed, out_specs=P(None, "row", "col"), check_vma=False
    )
```

```python
import functools
import math

import jax
import jax.numpy as jnp
from jax import lax
from jax.experimental import pallas as pl
from jax.experimental.pallas import tpu as pltpu
from jax.sharding import PartitionSpec as P

MESH = pl.DeviceIdType.MESH
F32, I32, BF16 = jnp.float32, jnp.int32, jnp.bfloat16

NY, NX, NZ, NCORE = 8, 4, 8, 2
NB = NX * NCORE
ROWS = 32
HALF = 16
GROUPS = 4
GROWS = HALF // GROUPS


def cos_sin(index, bits):
    size = 1 << bits
    index = index & (size - 1)
    quadrant = (index + (size >> 3)) >> (bits - 2)
    rest = index - (quadrant << (bits - 2))
    x = rest.astype(F32) * F32(2.0 * math.pi / size)
    y = x * x
    s = x * (1.0 + y * (-1.0 / 6 + y * (1.0 / 120 + y * (-1.0 / 5040 + y * (1.0 / 362880)))))
    c = 1.0 + y * (-0.5 + y * (1.0 / 24 + y * (-1.0 / 720 + y * (1.0 / 40320))))
    quadrant = quadrant & 3
    swap = (quadrant & 1) == 1
    cos = jnp.where(swap, s, c)
    sin = jnp.where(swap, c, s)
    cos = jnp.where((quadrant == 1) | (quadrant == 2), -cos, cos)
    sin = jnp.where(quadrant >= 2, -sin, sin)
    return cos, sin


def halves(value):
    high = value.astype(BF16)
    return high, (value - high.astype(F32)).astype(BF16)


def iota(shape, axis):
    return lax.broadcasted_iota(I32, shape, axis)


def rotation(cos, sin, part_out, part_in):
    cross = jnp.where(part_out == 0, sin, -sin)
    return jnp.where(part_out == part_in, cos, cross)


def phase(name):
    pass


def kernel(codes_in, aperture_in, offsets_in, out, codes, aperture, offsets, xslots, yslots, zslots, cslots,
           p1s, p1r, gathered, tcos, tsin, wmat, emat, zsend, zrecv, fsend, landing, turns,
           ready_y, ready_z, insem, p1send, p1recv, xsend, xrecv, ysend, yrecv, azsend, azrecv, csend, crecv,
           p2send, p2recv, asend, arecv, bsend, brecv):
    y = lax.axis_index("row")
    col = lax.axis_index("col")
    core = col % NCORE
    z = (col // NCORE) % NZ
    x = col // (NCORE * NZ)
    me = x * NCORE + core

    def at_y(k):
        return (k, col)

    def at_b(k):
        return (y, ((k // NCORE) * NZ + z) * NCORE + k % NCORE)

    def at_z(k):
        return (y, (x * NZ + k) * NCORE + core)

    def remote(src, dst, ss, rs, where):
        return pltpu.make_async_remote_copy(
            src_ref=src, dst_ref=dst, send_sem=ss, recv_sem=rs,
            device_id=where, device_id_type=MESH)

    phase("start")
    barrier = pltpu.get_barrier_semaphore()

    def signal(semaphore, where):
        pl.semaphore_signal(semaphore, inc=1, device_id=where, device_id_type=MESH)

    partners = [((x + dx) % NX) * NCORE + (core + dc) % NCORE
                for dx, dc in ((2, 0), (2, 1), (1, 0), (3, 0), (1, 1), (3, 1), (0, 1))]
    right, left = (z + 1) % NZ, (z + NZ - 1) % NZ
    for peer in partners:
        signal(barrier, at_b(peer))
    for peer in (right, left):
        signal(barrier, at_z(peer))
    for k in range(2, NZ - 1):
        peer = (z + k) % NZ

        @pl.when(peer > z)
        def _():
            signal(barrier, at_z(peer))

    @pl.loop(y + 1, NY)
    def _(k):
        signal(barrier, at_y(k))

    loads = [pltpu.make_async_copy(codes_in, codes, insem.at[0]),
             pltpu.make_async_copy(aperture_in, aperture, insem.at[1]),
             pltpu.make_async_copy(offsets_in, offsets, insem.at[2])]
    for load in loads:
        load.start()
    i, j = iota((512, 512), 0), iota((512, 512), 1)
    pick = jnp.where(i == 4 * (j & 127) + (j >> 7), 1.0, 0.0).astype(BF16)
    for load in loads:
        load.wait()

    phase("field")
    off0, off1 = offsets[:, 0:1], offsets[:, 1:2]
    opened = aperture[...]
    per_lane = jnp.sum(opened, axis=0, keepdims=True)
    count = sum(per_lane[:, j * 128:(j + 1) * 128] for j in range(4))
    total = jnp.broadcast_to(off0 + off1, (1, 128)).astype(F32)
    count = count.astype(F32)

    row = iota((ROWS, 512), 0)
    code = codes[...] + jnp.where(row < 16, off0, off0 + off1)
    code = code & 4095
    marked = jnp.concatenate([(code >> 6) + 64 * opened, code & 63], axis=0)
    moved = jnp.dot(marked.astype(F32).astype(BF16), pick, preferred_element_type=F32)
    moved = moved.astype(I32)
    high, low = moved[:ROWS], moved[ROWS:]
    amplitude = (high >> 6).astype(F32)
    cos, sin = cos_sin(((high & 63) << 6) + low, 12)
    field = (amplitude * cos, amplitude * sin)
    for b in range(NB):
        bx, bc = b // NCORE, b % NCORE
        for part in range(2):
            for g in range(GROUPS):
                first = bc * HALF + g * GROWS
                p1s[g, b * 8 + part * GROWS:b * 8 + (part + 1) * GROWS, :] = (
                    field[part][first:first + GROWS, bx * 128:(bx + 1) * 128])
    xslots[me, 0:1, :] = total
    xslots[me, 1:2, :] = count

    phase("barrier")
    entered_z = z - (z + 6) // 7 - z // 7
    pl.semaphore_wait(barrier, 9 + entered_z + y)

    phase("startp1")

    def p1_copy(g, peer):
        return remote(p1s.at[g, pl.ds(pl.multiple_of(peer * 8, 8), 8), :],
                      p1r.at[g, pl.ds(pl.multiple_of(me * 8, 8), 8), :],
                      p1send, p1recv.at[g], at_b(peer))

    for peer in partners:
        p1_copy(0, peer).start()
    for peer in partners:
        remote(xslots.at[me], xslots.at[me], xsend, xrecv, at_b(peer)).start()
    for g in range(1, GROUPS):
        for peer in partners:
            p1_copy(g, peer).start()
    for k in range(2, NZ - 1):
        peer = (z + k) % NZ

        @pl.when(peer < z)
        def _():
            signal(ready_z, at_z(peer))

    @pl.loop(0, y)
    def _(k):
        signal(ready_y, at_y(k))

    own = pl.ds(pl.multiple_of(me * 8, 8), 8)
    for g in range(GROUPS):
        p1r[g, own, :] = p1s[g, own, :]

    phase("tables")
    shape = (256, 192)
    i, j = iota(shape, 0), iota(shape, 1)
    for c in range(NCORE):
        a = ((j & 3) * NZ + ((j >> 3) & 7)) * NCORE + c
        cos, sin = cos_sin(a * (i & 127), 8)
        weight = rotation(cos, sin, i >> 7, (j >> 2) & 1)
        high = weight.astype(BF16).astype(F32)
        wmat[c] = jnp.where(j < 128, high, weight - high).astype(BF16)
    shape = (256, 128)
    cos, sin = cos_sin((4 * iota(shape, 1) + x) * iota(shape, 0), 17)
    tcos[...] = cos
    tsin[...] = sin
    shape = (32, 256)
    i, j = iota(shape, 0), iota(shape, 1)
    q = 2 * (i >> 3) + ((i >> 1) & 1)
    d_low = NCORE * z + ((i >> 2) & 1)
    cos, sin = cos_sin((4 * (j & 127) + x) * (8 * d_low + q), 9)
    e_high, e_low = halves(rotation(cos, sin, i & 1, j >> 7))
    emat[0:32, :] = e_high
    emat[32:64, :] = e_low

    def receive(g):
        messages = p1r.at[g, pl.ds(0, 56), :]
        remote(messages, messages, p1send, p1recv.at[g], at_z(right)).wait_recv()
        for n in range(GROWS):
            for c in range(NCORE):
                for part in range(2):
                    spot = c * 8 + part * NX
                    gathered[z, g * GROWS + n, spot:spot + NX, :] = (
                        p1r[g, pl.ds(c * 8 + part * GROWS + n, NX, stride=8 * NCORE), :])

    def ring(block, group, way, step):
        part = gathered.at[block, pl.ds(group * GROWS, GROWS)]
        return remote(part, part, p2send, p2recv.at[block, group],
                      at_z(right if way == 0 else left))

    def ring_block(way, step):
        return (z + NZ - step) % NZ if way == 0 else (z + step) % NZ

    def forwards(way, step, group):
        return step < 3 or (group % 2 == 0) == (way == 0)

    def arrived(block, group):
        part = gathered.at[block, pl.ds(group * GROWS, GROWS)]
        remote(part, part, p2send, p2recv.at[block, group],
               at_z(left)).wait_recv()

    def ring_step(step, group):
        if step == 0:
            receive(group)
        for way in range(2):
            if step:
                arrived(ring_block(way, step), group)
            if forwards(way, step, group):
                ring(ring_block(way, step), group, way, step).start()

    def y_copy(peer, slot):
        return remote(yslots.at[slot], yslots.at[slot], ysend.at[peer], yrecv.at[slot], at_y(peer))

    def az_copy(peer):
        return remote(zslots.at[z], zslots.at[z], azsend, azrecv, at_z(peer))

    def c_copy(peer):
        return remote(cslots.at[y], cslots.at[y], csend, crecv, at_y(peer))

    def small_y():
        remote(xslots.at[pl.ds(0, 7)], xslots.at[pl.ds(0, 7)], xsend, xrecv, at_z(right)).wait_recv()
        for k in range(NB):
            yslots[y, k:k + 1, :] = xslots[k % NX * NCORE + k // NX, 0:1, :]
        @pl.when(y < NY - 1)
        def _():
            pl.semaphore_wait(ready_y, NY - 1 - y)

        @pl.loop(y + 1, NY)
        def _(k):
            y_copy(k, y).start()

    def small_z():
        @pl.loop(0, y)
        def _(k):
            y_copy(k, k).wait_recv()
        before = lax.fori_loop(0, y, lambda k, acc: acc + yslots[k], jnp.zeros((NB, 128), F32))
        shape = (NB, 128)
        diagonal = jnp.where(iota(shape, 0) == (iota(shape, 1) & 7), before, 0.0)
        zslots[z, 0:1, :] = jnp.sum(diagonal, axis=0, keepdims=True)
        zslots[z, 1:2, :] = jnp.sum(xslots[:, 1, :], axis=0, keepdims=True)
        @pl.when(z < NZ - 2)
        def _():
            pl.semaphore_wait(ready_z, 5 + (z + 6) // 7 - z)

        @pl.loop(1, NZ)
        def _(k):
            az_copy((z + k) % NZ).start()

    known = []

    def prefix():
        remote(zslots.at[pl.ds(0, 7)], zslots.at[pl.ds(0, 7)], azsend, azrecv, at_z(right)).wait_recv()
        shape = (NZ, 8, 128)
        sublane, lane = iota(shape, 1), iota(shape, 2)
        sign = jnp.where(sublane < NX, F32(-1.0), F32(1.0))
        every = jnp.broadcast_to(zslots[:, 0:1, :], shape)
        for c in range(NCORE):
            mine = jnp.where(lane == c * NX + (sublane & 3), every, 0.0)
            before = jnp.broadcast_to(jnp.sum(mine, axis=2, keepdims=True), shape)
            cos, sin = cos_sin(before.astype(I32), 12)
            turns[c, 0] = cos
            turns[c, 1] = sin * sign
        cslots[y] = zslots[:, 1, :]

        @pl.loop(1, NY)
        def _(k):
            c_copy((y + k) % NY).start()

    def normalization():
        remote(cslots.at[pl.ds(0, 7)], cslots.at[pl.ds(0, 7)], csend, crecv, at_z(right)).wait_recv()
        total = jnp.sum(cslots[...], axis=0)
        total = jnp.sum(jnp.sum(total, axis=0, keepdims=True), axis=1, keepdims=True)
        known.append(jnp.sqrt(F32(ROWS * NY) / total))

    nt = (((1,), (1,)), ((), ()))

    def a_copy(g, peer):
        return remote(zsend.at[g, :, pl.ds(peer * 8 * GROWS, 8 * GROWS), :], zrecv.at[x, g],
                      asend, arecv.at[g], at_b(peer * NCORE + core))

    def transform(g):
        for pair in range(GROWS // 2):
            parity = []
            for c in range(NCORE):
                columns = []
                for n in range(2):
                    block = gathered[:, g * GROWS + pair * 2 + n, c * 8:(c + 1) * 8, :]
                    turned = block * turns[c, 0] + pltpu.roll(block, NX, axis=1) * turns[c, 1]
                    columns.append(turned.reshape(64, 128))
                high, low = halves(jnp.concatenate(columns, axis=1))
                parity.append(jnp.dot(wmat[c], jnp.concatenate([high, low, high], axis=0),
                                      preferred_element_type=F32))
            for h, spec in enumerate((parity[0] + parity[1], parity[0] - parity[1])):
                c, s = tcos[h * 128:(h + 1) * 128, :], tsin[h * 128:(h + 1) * 128, :]
                for n in range(2):
                    re = spec[0:128, n * 128:(n + 1) * 128]
                    im = spec[128:256, n * 128:(n + 1) * 128]
                    turned = jnp.concatenate([re * c + im * s, im * c - re * s], axis=1)
                    high, low = halves(turned)
                    first = lax.dot_general(emat[...], high, nt, preferred_element_type=F32)
                    second = lax.dot_general(emat[0:32, :], low, nt, preferred_element_type=F32)
                    zsend[g, h, pl.ds(pair * 2 + n, 32, stride=GROWS), :] = (
                        first[0:32] + first[32:64] + second)

    def finish(first, last):
        if first == 0:
            prefix()

        @pl.loop(first, last)
        def _(g):
            arrived((z + 4) % NZ, g)
            transform(g)
            for k in (2, 1, 3):
                a_copy(g, (x + k) % NX).start()
            zrecv[x, g] = zsend[g, :, pl.ds(pl.multiple_of(x * 8 * GROWS, 8 * GROWS), 8 * GROWS), :]

    def b_copy(g, peer):
        return remote(fsend.at[g, peer],
                      landing.at[core, g, :, pl.ds(pl.multiple_of(x * 512, 512), 512)],
                      bsend, brecv.at[g], at_b(peer))

    def combine(g):
        remote(zrecv.at[pl.ds(0, 3), g], zrecv.at[pl.ds(0, 3), g], asend, arecv.at[g],
               at_z(right)).wait_recv()
        turn = jnp.where(iota((8, 128), 0) < GROWS, F32(1.0), F32(-1.0))
        for dc in range(2):
            for ql in range(2):
                for h in range(2):
                    start = (dc * 2 + ql) * 8
                    t = [zrecv[b, g, h, start:start + 8, :] for b in range(NX)]
                    even, odd = t[0] + t[2], t[1] + t[3]
                    differ = t[0] - t[2]
                    turned = pltpu.roll(t[1] - t[3], GROWS, axis=0) * turn
                    results = (even + odd, differ + turned, even - odd, differ - turned)
                    for dx in range(NX):
                        fsend[g, dx * NCORE + dc, :, (ql * 2 + h) * 128:(ql * 2 + h + 1) * 128] = results[dx]

        for peer in partners:
            b_copy(g, peer).start()
        landing[core, g, :, pl.ds(pl.multiple_of(x * 512, 512), 512)] = fsend[g, me]

    def deliver(g):
        remote(fsend.at[g, pl.ds(0, 7)], fsend.at[g, pl.ds(0, 7)], bsend, brecv.at[g],
               at_z(right)).wait_recv()
        scale = known[0]
        for c in range(NCORE):
            for p in range(2):
                out[p, pl.ds(c * HALF + g * GROWS, GROWS), :] = (
                    landing[c, g, p * GROWS:(p + 1) * GROWS, :] * scale)

    for _, name, work in sorted(schedule(ring_step, finish, small_y, small_z), key=lambda e: e[0]):
        phase(name)
        work()

    phase("combine")
    pl.loop(0, GROUPS)(combine)
    phase("cwait")
    normalization()
    phase("deliver")
    if LOOP_OUT:
        pl.loop(0, GROUPS)(deliver)
    else:
        for g in range(GROUPS):
            deliver(g)

    phase("drain")

    @pl.loop(y + 1, NY)
    def _(k):
        y_copy(k, y).wait_send()

    for ref, semaphore in ((p1s.at[:, pl.ds(0, 56), :], p1send), (xslots.at[pl.ds(0, 7)], xsend),
                           (zslots.at[pl.ds(0, 7)], azsend),
                           (cslots.at[pl.ds(0, 7)], csend), (gathered.at[pl.ds(0, 7)], p2send),
                           (zrecv.at[pl.ds(0, 3)], asend), (fsend.at[:, pl.ds(0, 7)], bsend)):
        remote(ref, ref, semaphore, xrecv, at_z(right)).wait_send()
    phase(None)


def schedule(ring_step, finish, small_y, small_z):
    part = functools.partial
    events = [(SMALL[0], "ysmall", small_y), (SMALL[1], "zsmall", small_z)]
    for g in range(GROUPS):
        for step in range(4):
            events.append((RING[step] + g * LAG, f"r{step}{g}", part(ring_step, step, g)))
    for k in range(len(FIN)):
        first, when = FIN[k]
        last = FIN[k + 1][0] if k + 1 < len(FIN) else GROUPS
        events.append((when, f"fin{first}", part(finish, first, last)))
    return events


RING = (0.0, 2.2, 4.4, 6.6)
LAG = 1.0
SMALL = (2.3, 6.0)
FIN = ((0, 8.8), (1, 10.0))
LOOP_OUT = False


def per_device(phase_codes, aperture, tile_offsets):
    dma = pltpu.SemaphoreType.DMA
    vmem = pltpu.VMEM
    return pl.pallas_call(
        kernel,
        out_shape=pltpu.VMEM((2, ROWS, 2048), F32),
        in_specs=[pl.BlockSpec(memory_space=pl.ANY)] * 3,
        out_specs=pl.BlockSpec(memory_space=pltpu.VMEM),
        scratch_shapes=[
            vmem((ROWS, 512), I32), vmem((ROWS, 512), I32), vmem((1, 2), I32),
            vmem((NB, 2, 128), F32), vmem((NY, NB, 128), F32), vmem((NZ, 2, 128), F32), vmem((NY, NB, 128), F32),
            vmem((GROUPS, NB * 8, 128), F32), vmem((GROUPS, NB * 8, 128), F32),
            vmem((NZ, HALF, 16, 128), F32),
            vmem((256, 128), F32), vmem((256, 128), F32),
            vmem((NCORE, 256, 192), BF16), vmem((64, 256), BF16),
            vmem((GROUPS, 2, 32 * GROWS, 128), F32),
            vmem((NX, GROUPS, 2, 8 * GROWS, 128), F32),
            vmem((GROUPS, NB, 2 * GROWS, 512), F32),
            vmem((NCORE, GROUPS, 2 * GROWS, 2048), F32),
            vmem((NCORE, 2, NZ, 8, 128), F32),
            pltpu.SemaphoreType.REGULAR, pltpu.SemaphoreType.REGULAR, dma((3,)),
            dma, dma((GROUPS,)), dma, dma, dma((NY,)), dma((NY,)), dma, dma, dma, dma,
            dma, dma((NZ, GROUPS)), dma, dma((GROUPS,)), dma, dma((GROUPS,)),
        ],
        compiler_params=pltpu.CompilerParams(collective_id=0, has_side_effects=True),
    )(phase_codes, aperture, tile_offsets.reshape(1, 2))


def solution(mesh):
    placed = (P("row", "col"), P("row", "col"), P("row", "col"))
    return jax.shard_map(
        per_device, mesh=mesh, in_specs=placed, out_specs=P(None, "row", "col"), check_vma=False
    )
```

```python
import functools
import math

import jax
import jax.numpy as jnp
from jax import lax
from jax.experimental import pallas as pl
from jax.experimental.pallas import tpu as pltpu
from jax.sharding import PartitionSpec as P

MESH = pl.DeviceIdType.MESH
F32, I32, BF16 = jnp.float32, jnp.int32, jnp.bfloat16

NY, NX, NZ, NCORE = 8, 4, 8, 2
NB = NX * NCORE
ROWS = 32
HALF = 16
GROUPS = 4
GROWS = HALF // GROUPS


def cos_sin(index, bits):
    size = 1 << bits
    index = index & (size - 1)
    quadrant = (index + (size >> 3)) >> (bits - 2)
    rest = index - (quadrant << (bits - 2))
    x = rest.astype(F32) * F32(2.0 * math.pi / size)
    y = x * x
    s = x * (1.0 + y * (-1.0 / 6 + y * (1.0 / 120 + y * (-1.0 / 5040 + y * (1.0 / 362880)))))
    c = 1.0 + y * (-0.5 + y * (1.0 / 24 + y * (-1.0 / 720 + y * (1.0 / 40320))))
    quadrant = quadrant & 3
    swap = (quadrant & 1) == 1
    cos = jnp.where(swap, s, c)
    sin = jnp.where(swap, c, s)
    cos = jnp.where((quadrant == 1) | (quadrant == 2), -cos, cos)
    sin = jnp.where(quadrant >= 2, -sin, sin)
    return cos, sin


def halves(value):
    high = value.astype(BF16)
    return high, (value - high.astype(F32)).astype(BF16)


def iota(shape, axis):
    return lax.broadcasted_iota(I32, shape, axis)


def rotation(cos, sin, part_out, part_in):
    cross = jnp.where(part_out == 0, sin, -sin)
    return jnp.where(part_out == part_in, cos, cross)


def phase(name):
    pass


def kernel(codes_in, aperture_in, offsets_in, out, codes, aperture, offsets, xslots, yslots, zslots, cslots,
           p1s, p1r, gathered, tcos, tsin, wmat, emat, zsend, zrecv, fsend, landing,
           ready_y, ready_z, insem, p1send, p1recv, xsend, xrecv, ysend, yrecv, azsend, azrecv, csend, crecv,
           p2send, p2recv, asend, arecv, bsend, brecv):
    y = lax.axis_index("row")
    col = lax.axis_index("col")
    core = col % NCORE
    z = (col // NCORE) % NZ
    x = col // (NCORE * NZ)
    me = x * NCORE + core

    def at_y(k):
        return (k, col)

    def at_b(k):
        return (y, ((k // NCORE) * NZ + z) * NCORE + k % NCORE)

    def at_z(k):
        return (y, (x * NZ + k) * NCORE + core)

    def remote(src, dst, ss, rs, where):
        return pltpu.make_async_remote_copy(
            src_ref=src, dst_ref=dst, send_sem=ss, recv_sem=rs,
            device_id=where, device_id_type=MESH)

    phase("start")
    barrier = pltpu.get_barrier_semaphore()

    def signal(semaphore, where):
        pl.semaphore_signal(semaphore, inc=1, device_id=where, device_id_type=MESH)

    partners = [((x + dx) % NX) * NCORE + (core + dc) % NCORE
                for dx, dc in ((2, 0), (2, 1), (1, 0), (3, 0), (1, 1), (3, 1), (0, 1))]
    right, left = (z + 1) % NZ, (z + NZ - 1) % NZ
    for peer in partners:
        signal(barrier, at_b(peer))
    for peer in (right, left):
        signal(barrier, at_z(peer))
    for k in range(2, NZ - 1):
        peer = (z + k) % NZ

        @pl.when(peer > z)
        def _():
            signal(barrier, at_z(peer))

    @pl.loop(y + 1, NY)
    def _(k):
        signal(barrier, at_y(k))

    loads = [pltpu.make_async_copy(codes_in, codes, insem.at[0]),
             pltpu.make_async_copy(aperture_in, aperture, insem.at[1]),
             pltpu.make_async_copy(offsets_in, offsets, insem.at[2])]
    for load in loads:
        load.start()
    i, j = iota((512, 512), 0), iota((512, 512), 1)
    pick = jnp.where(i == 4 * (j & 127) + (j >> 7), 1.0, 0.0).astype(BF16)
    for load in loads:
        load.wait()

    phase("field")
    off0, off1 = offsets[:, 0:1], offsets[:, 1:2]
    opened = aperture[...]
    per_lane = jnp.sum(opened, axis=0, keepdims=True)
    count = sum(per_lane[:, j * 128:(j + 1) * 128] for j in range(4))
    total = jnp.broadcast_to(off0 + off1, (1, 128)).astype(F32)
    count = count.astype(F32)

    row = iota((ROWS, 512), 0)
    code = codes[...] + jnp.where(row < 16, off0, off0 + off1)
    code = code & 4095
    marked = jnp.concatenate([(code >> 6) + 64 * opened, code & 63], axis=0)
    moved = jnp.dot(marked.astype(F32).astype(BF16), pick, preferred_element_type=F32)
    moved = moved.astype(I32)
    high, low = moved[:ROWS], moved[ROWS:]
    amplitude = (high >> 6).astype(F32)
    cos, sin = cos_sin(((high & 63) << 6) + low, 12)
    field = (amplitude * cos, amplitude * sin)
    for b in range(NB):
        bx, bc = b // NCORE, b % NCORE
        for part in range(2):
            for g in range(GROUPS):
                first = bc * HALF + g * GROWS
                p1s[g, b * 8 + part * GROWS:b * 8 + (part + 1) * GROWS, :] = (
                    field[part][first:first + GROWS, bx * 128:(bx + 1) * 128])
    xslots[me, 0:1, :] = total
    xslots[me, 1:2, :] = count

    phase("barrier")
    entered_z = z - (z + 6) // 7 - z // 7
    pl.semaphore_wait(barrier, 9 + entered_z + y)

    phase("startp1")

    def p1_copy(g, peer):
        return remote(p1s.at[g, pl.ds(pl.multiple_of(peer * 8, 8), 8), :],
                      p1r.at[g, pl.ds(pl.multiple_of(me * 8, 8), 8), :],
                      p1send, p1recv.at[g], at_b(peer))

    for peer in partners:
        p1_copy(0, peer).start()
    for peer in partners:
        remote(xslots.at[me], xslots.at[me], xsend, xrecv, at_b(peer)).start()
    for g in range(1, GROUPS):
        for peer in partners:
            p1_copy(g, peer).start()
    for k in range(2, NZ - 1):
        peer = (z + k) % NZ

        @pl.when(peer < z)
        def _():
            signal(ready_z, at_z(peer))

    @pl.loop(0, y)
    def _(k):
        signal(ready_y, at_y(k))

    own = pl.ds(pl.multiple_of(me * 8, 8), 8)
    for g in range(GROUPS):
        p1r[g, own, :] = p1s[g, own, :]

    phase("tables")
    shape = (256, 192)
    i, j = iota(shape, 0), iota(shape, 1)
    for c in range(NCORE):
        a = ((j & 3) * NZ + ((j >> 3) & 7)) * NCORE + c
        cos, sin = cos_sin(a * (i & 127), 8)
        weight = rotation(cos, sin, i >> 7, (j >> 2) & 1)
        high = weight.astype(BF16).astype(F32)
        wmat[c] = jnp.where(j < 128, high, weight - high).astype(BF16)
    shape = (256, 128)
    cos, sin = cos_sin((4 * iota(shape, 1) + x) * iota(shape, 0), 17)
    tcos[...] = cos
    tsin[...] = sin
    shape = (32, 256)
    i, j = iota(shape, 0), iota(shape, 1)
    q = 2 * (i >> 3) + ((i >> 1) & 1)
    d_low = NCORE * z + ((i >> 2) & 1)
    cos, sin = cos_sin((4 * (j & 127) + x) * (8 * d_low + q), 9)
    e_high, e_low = halves(rotation(cos, sin, i & 1, j >> 7))
    emat[0:32, :] = e_high
    emat[32:64, :] = e_low

    def receive(g):
        messages = p1r.at[g, pl.ds(0, 56), :]
        remote(messages, messages, p1send, p1recv.at[g], at_z(right)).wait_recv()
        for n in range(GROWS):
            for c in range(NCORE):
                for part in range(2):
                    spot = c * 8 + part * NX
                    gathered[z, g * GROWS + n, spot:spot + NX, :] = (
                        p1r[g, pl.ds(c * 8 + part * GROWS + n, NX, stride=8 * NCORE), :])

    def ring(block, group, way, step):
        part = gathered.at[block, pl.ds(group * GROWS, GROWS)]
        return remote(part, part, p2send, p2recv.at[block, group],
                      at_z(right if way == 0 else left))

    def ring_block(way, step):
        return (z + NZ - step) % NZ if way == 0 else (z + step) % NZ

    def forwards(way, step, group):
        return step < 3 or (group % 2 == 0) == (way == 0)

    def arrived(block, group):
        part = gathered.at[block, pl.ds(group * GROWS, GROWS)]
        remote(part, part, p2send, p2recv.at[block, group],
               at_z(left)).wait_recv()

    def ring_step(step, group):
        if step == 0:
            receive(group)
        for way in range(2):
            if step:
                arrived(ring_block(way, step), group)
            if forwards(way, step, group):
                ring(ring_block(way, step), group, way, step).start()

    def y_copy(peer, slot):
        return remote(yslots.at[slot], yslots.at[slot], ysend.at[peer], yrecv.at[slot], at_y(peer))

    def az_copy(peer):
        return remote(zslots.at[z], zslots.at[z], azsend, azrecv, at_z(peer))

    def c_copy(peer):
        return remote(cslots.at[y], cslots.at[y], csend, crecv, at_y(peer))

    def small_y():
        remote(xslots.at[pl.ds(0, 7)], xslots.at[pl.ds(0, 7)], xsend, xrecv, at_z(right)).wait_recv()
        for k in range(NB):
            yslots[y, k:k + 1, :] = xslots[k % NX * NCORE + k // NX, 0:1, :]
        @pl.when(y < NY - 1)
        def _():
            pl.semaphore_wait(ready_y, NY - 1 - y)

        @pl.loop(y + 1, NY)
        def _(k):
            y_copy(k, y).start()

    def small_z():
        @pl.loop(0, y)
        def _(k):
            y_copy(k, k).wait_recv()
        before = lax.fori_loop(0, y, lambda k, acc: acc + yslots[k], jnp.zeros((NB, 128), F32))
        shape = (NB, 128)
        diagonal = jnp.where(iota(shape, 0) == (iota(shape, 1) & 7), before, 0.0)
        zslots[z, 0:1, :] = jnp.sum(diagonal, axis=0, keepdims=True)
        zslots[z, 1:2, :] = jnp.sum(xslots[:, 1, :], axis=0, keepdims=True)
        @pl.when(z < NZ - 2)
        def _():
            pl.semaphore_wait(ready_z, 5 + (z + 6) // 7 - z)

        @pl.loop(1, NZ)
        def _(k):
            az_copy((z + k) % NZ).start()

    known = []

    def prefix():
        remote(zslots.at[pl.ds(0, 7)], zslots.at[pl.ds(0, 7)], azsend, azrecv, at_z(right)).wait_recv()
        shape = (NZ, 8, 128)
        sublane, lane = iota(shape, 1), iota(shape, 2)
        sign = jnp.where(sublane < NX, F32(-1.0), F32(1.0))
        every = jnp.broadcast_to(zslots[:, 0:1, :], shape)
        turns = []
        for c in range(NCORE):
            mine = jnp.where(lane == c * NX + (sublane & 3), every, 0.0)
            before = jnp.broadcast_to(jnp.sum(mine, axis=2, keepdims=True), shape)
            cos, sin = cos_sin(before.astype(I32), 12)
            turns.append((cos, sin * sign))
        known.append(turns)
        cslots[y] = zslots[:, 1, :]

        @pl.loop(1, NY)
        def _(k):
            c_copy((y + k) % NY).start()

    def normalization():
        remote(cslots.at[pl.ds(0, 7)], cslots.at[pl.ds(0, 7)], csend, crecv, at_z(right)).wait_recv()
        total = jnp.sum(cslots[...], axis=0)
        total = jnp.sum(jnp.sum(total, axis=0, keepdims=True), axis=1, keepdims=True)
        known.append(jnp.sqrt(F32(ROWS * NY) / total))

    nt = (((1,), (1,)), ((), ()))

    def a_copy(g, peer):
        return remote(zsend.at[g, :, pl.ds(peer * 8 * GROWS, 8 * GROWS), :], zrecv.at[x, g],
                      asend, arecv.at[g], at_b(peer * NCORE + core))

    def transform(g):
        for pair in range(GROWS // 2):
            parity = []
            for c in range(NCORE):
                cos, sin = known[0][c]
                columns = []
                for n in range(2):
                    block = gathered[:, g * GROWS + pair * 2 + n, c * 8:(c + 1) * 8, :]
                    columns.append((block * cos + pltpu.roll(block, NX, axis=1) * sin).reshape(64, 128))
                high, low = halves(jnp.concatenate(columns, axis=1))
                parity.append(jnp.dot(wmat[c], jnp.concatenate([high, low, high], axis=0),
                                      preferred_element_type=F32))
            for h, spec in enumerate((parity[0] + parity[1], parity[0] - parity[1])):
                c, s = tcos[h * 128:(h + 1) * 128, :], tsin[h * 128:(h + 1) * 128, :]
                for n in range(2):
                    re = spec[0:128, n * 128:(n + 1) * 128]
                    im = spec[128:256, n * 128:(n + 1) * 128]
                    turned = jnp.concatenate([re * c + im * s, im * c - re * s], axis=1)
                    high, low = halves(turned)
                    first = lax.dot_general(emat[...], high, nt, preferred_element_type=F32)
                    second = lax.dot_general(emat[0:32, :], low, nt, preferred_element_type=F32)
                    zsend[g, h, pl.ds(pair * 2 + n, 32, stride=GROWS), :] = (
                        first[0:32] + first[32:64] + second)

    def finish(first, last):
        if first == 0:
            prefix()

        @pl.loop(first, last)
        def _(g):
            arrived((z + 4) % NZ, g)
            transform(g)
            for k in (2, 1, 3):
                a_copy(g, (x + k) % NX).start()
            zrecv[x, g] = zsend[g, :, pl.ds(pl.multiple_of(x * 8 * GROWS, 8 * GROWS), 8 * GROWS), :]

    def b_copy(g, peer):
        return remote(fsend.at[g, peer],
                      landing.at[core, g, :, pl.ds(pl.multiple_of(x * 512, 512), 512)],
                      bsend, brecv.at[g], at_b(peer))

    def combine(g):
        remote(zrecv.at[pl.ds(0, 3), g], zrecv.at[pl.ds(0, 3), g], asend, arecv.at[g],
               at_z(right)).wait_recv()
        turn = jnp.where(iota((8, 128), 0) < GROWS, F32(1.0), F32(-1.0))
        for dc in range(2):
            for ql in range(2):
                for h in range(2):
                    start = (dc * 2 + ql) * 8
                    t = [zrecv[b, g, h, start:start + 8, :] for b in range(NX)]
                    even, odd = t[0] + t[2], t[1] + t[3]
                    differ = t[0] - t[2]
                    turned = pltpu.roll(t[1] - t[3], GROWS, axis=0) * turn
                    results = (even + odd, differ + turned, even - odd, differ - turned)
                    for dx in range(NX):
                        fsend[g, dx * NCORE + dc, :, (ql * 2 + h) * 128:(ql * 2 + h + 1) * 128] = results[dx]

        for peer in partners:
            b_copy(g, peer).start()
        landing[core, g, :, pl.ds(pl.multiple_of(x * 512, 512), 512)] = fsend[g, me]

    def deliver(g):
        remote(fsend.at[g, pl.ds(0, 7)], fsend.at[g, pl.ds(0, 7)], bsend, brecv.at[g],
               at_z(right)).wait_recv()
        scale = known[1]
        for c in range(NCORE):
            for p in range(2):
                out[p, pl.ds(c * HALF + g * GROWS, GROWS), :] = (
                    landing[c, g, p * GROWS:(p + 1) * GROWS, :] * scale)

    for _, name, work in sorted(schedule(ring_step, finish, small_y, small_z), key=lambda e: e[0]):
        phase(name)
        work()

    phase("combine")
    pl.loop(0, GROUPS)(combine)
    phase("cwait")
    normalization()
    phase("deliver")
    if LOOP_OUT:
        pl.loop(0, GROUPS)(deliver)
    else:
        for g in range(GROUPS):
            deliver(g)

    phase("drain")

    @pl.loop(y + 1, NY)
    def _(k):
        y_copy(k, y).wait_send()

    for ref, semaphore in ((p1s.at[:, pl.ds(0, 56), :], p1send), (xslots.at[pl.ds(0, 7)], xsend),
                           (zslots.at[pl.ds(0, 7)], azsend),
                           (cslots.at[pl.ds(0, 7)], csend), (gathered.at[pl.ds(0, 7)], p2send),
                           (zrecv.at[pl.ds(0, 3)], asend), (fsend.at[:, pl.ds(0, 7)], bsend)):
        remote(ref, ref, semaphore, xrecv, at_z(right)).wait_send()
    phase(None)


def schedule(ring_step, finish, small_y, small_z):
    part = functools.partial
    events = [(SMALL[0], "ysmall", small_y), (SMALL[1], "zsmall", small_z)]
    for g in range(GROUPS):
        for step in range(4):
            events.append((RING[step] + g * LAG, f"r{step}{g}", part(ring_step, step, g)))
    for k in range(len(FIN)):
        first, when = FIN[k]
        last = FIN[k + 1][0] if k + 1 < len(FIN) else GROUPS
        events.append((when, f"fin{first}", part(finish, first, last)))
    return events


RING = (0.0, 2.2, 4.4, 6.6)
LAG = 1.0
SMALL = (2.3, 5.3)
FIN = ((0, 8.8), (1, 10.0))
LOOP_OUT = False


def per_device(phase_codes, aperture, tile_offsets):
    dma = pltpu.SemaphoreType.DMA
    vmem = pltpu.VMEM
    return pl.pallas_call(
        kernel,
        out_shape=pltpu.VMEM((2, ROWS, 2048), F32),
        in_specs=[pl.BlockSpec(memory_space=pl.ANY)] * 3,
        out_specs=pl.BlockSpec(memory_space=pltpu.VMEM),
        scratch_shapes=[
            vmem((ROWS, 512), I32), vmem((ROWS, 512), I32), vmem((1, 2), I32),
            vmem((NB, 2, 128), F32), vmem((NY, NB, 128), F32), vmem((NZ, 2, 128), F32), vmem((NY, NB, 128), F32),
            vmem((GROUPS, NB * 8, 128), F32), vmem((GROUPS, NB * 8, 128), F32),
            vmem((NZ, HALF, 16, 128), F32),
            vmem((256, 128), F32), vmem((256, 128), F32),
            vmem((NCORE, 256, 192), BF16), vmem((64, 256), BF16),
            vmem((GROUPS, 2, 32 * GROWS, 128), F32),
            vmem((NX, GROUPS, 2, 8 * GROWS, 128), F32),
            vmem((GROUPS, NB, 2 * GROWS, 512), F32),
            vmem((NCORE, GROUPS, 2 * GROWS, 2048), F32),
            pltpu.SemaphoreType.REGULAR, pltpu.SemaphoreType.REGULAR, dma((3,)),
            dma, dma((GROUPS,)), dma, dma, dma((NY,)), dma((NY,)), dma, dma, dma, dma,
            dma, dma((NZ, GROUPS)), dma, dma((GROUPS,)), dma, dma((GROUPS,)),
        ],
        compiler_params=pltpu.CompilerParams(collective_id=0, has_side_effects=True),
    )(phase_codes, aperture, tile_offsets.reshape(1, 2))


def solution(mesh):
    placed = (P("row", "col"), P("row", "col"), P("row", "col"))
    return jax.shard_map(
        per_device, mesh=mesh, in_specs=placed, out_specs=P(None, "row", "col"), check_vma=False
    )
```
